32 devices in a mesh: dp: 8 (over z, x), tensor: 4 (over y, core).
Axes of the slice: x: 2, y: 2, z: 4, core: 2. Of those that a mesh axis runs over, the one named last changes fastest.
Arguments:
- tokens: bfloat16 [16, 512, 768], P('dp'), may hold values from -6 to 6
- lengths: int32 [16], P('dp'), may hold values from 1 to 512, 2048 in all
- groups: int32 [16, 512], P('dp'), may hold values from 0 to 3, never falling along the last dimension, each value on 1 to 256 neighbouring positions
- key_mask: int32 [16, 512], P('dp'), may hold values 0 or 1
- w_query: bfloat16 [768, 768], P(None, 'tensor'), may hold values from -0.21875 to 0.21875
- b_query: float32 [768], P('tensor'), may hold values from -3 to 3
- w_key: bfloat16 [768, 768], P(None, 'tensor'), may hold values from -0.21875 to 0.21875
- w_value: bfloat16 [768, 768], P(None, 'tensor'), may hold values from -0.21875 to 0.21875
- b_value: float32 [768], P('tensor'), may hold values from -3 to 3
- rel_bias: float32 [12, 256], P('tensor'), may hold values from -4 to 4
- w_out: bfloat16 [768, 768], P('tensor'), may hold values from -0.625 to 0.625
- b_out: float32 [768], replicated, may hold values from -3 to 3
- gain_one: float32 [768], replicated, may hold values from 0.25 to 1.75
- shift_one: float32 [768], replicated, may hold values from -3 to 3
- w_inner: bfloat16 [768, 3072], P(None, 'tensor'), may hold values from -0.21875 to 0.21875
- b_inner: float32 [3072], P('tensor'), may hold values from -3 to 3
- w_outer: bfloat16 [3072, 768], P('tensor'), may hold values from -0.109375 to 0.109375
- b_outer: float32 [768], replicated, may hold values from -3 to 3
- gain_two: float32 [768], replicated, may hold values from 0.25 to 1.75
- shift_two: float32 [768], replicated, may hold values from -3 to 3
- cotangent: bfloat16 [16, 256, 768], P('dp'), may hold values from -24 to 24
Outputs:
- output: bfloat16 [16, 256, 768], P('dp')
- grad_tokens: bfloat16 [16, 512, 768], P('dp')
- grad_w_query: float32 [768, 768], P(None, 'tensor')
- grad_b_query: float32 [768], P('tensor')
- grad_w_key: float32 [768, 768], P(None, 'tensor')
- grad_w_value: float32 [768, 768], P(None, 'tensor')
- grad_b_value: float32 [768], P('tensor')
- grad_rel_bias: float32 [12, 256], P('tensor')
- grad_w_out: float32 [768, 768], P('tensor')
- grad_b_out: float32 [768], replicated
- grad_gain_one: float32 [768], replicated
- grad_shift_one: float32 [768], replicated
- grad_w_inner: float32 [768, 3072], P(None, 'tensor')
- grad_b_inner: float32 [3072], P('tensor')
- grad_w_outer: float32 [3072, 768], P('tensor')
- grad_b_outer: float32 [768], replicated
- grad_gain_two: float32 [768], replicated
- grad_shift_two: float32 [768], replicated
The draws below stay inside these ranges and needn't reach their ends.
Inputs may be any that keep to these rules, and one draw needn't show every extreme that they name: `lengths`: the longest row has exactly 512 used tokens. `groups`: document ids never fall along a row; a document has at most half of 512 positions.
All inputs are finite; a program needn't handle non-finite values. No bound on the sum of `lengths` or of `key_mask` on one device may be relied on, other than what follows from the above.
Results may differ from the reference program's by a relative error of at most 0.013.
Values sent between devices are 32-bit elements; how exact they have to be, the bound alone decides.
No kernel may reach another device: no remote copies, remote signals or barrier semaphores. Data moves between devices by JAX's collectives and lax.ppermute only.
A program may use at most 128 MiB of HBM per device.

```python
import math
import jax
import jax.numpy as jnp
import numpy as np
from jax import lax

D = 768
H = 12
DH = 64
FF = 3072
L = 512
NREL = 256
SEGS = 4
ROWS = 16


def draw_cotangent(key, part):
    rising = 3.0 ** (jnp.arange(ROWS, dtype=jnp.float32) / max(ROWS - 1, 1))
    base = jnp.clip(jax.random.normal(key, (ROWS, L // 2, D), jnp.float32), -8.0, 8.0)
    return (base * rising[:, None, None]).astype(jnp.bfloat16)


def set_ends(drawn, rng, smallest, top_value):
    place = [jax.random.randint(jax.random.fold_in(rng, axis), (), 0, length) for axis, length in enumerate(drawn.shape)]
    longest = drawn.shape.index(max(drawn.shape))
    beside = place[:longest] + [(place[longest] + 1) % drawn.shape[longest]] + place[longest + 1:]
    return drawn.at[tuple(place)].set(smallest).at[tuple(beside)].set(top_value)


def shard_levels(rng, extent, shards, least, largest):
    loudness = 1.0
    for dim, blocks in shards:
        heights = jax.random.uniform(jax.random.fold_in(jax.random.fold_in(rng, 6), dim), (blocks,), jnp.float32, least / len(shards), largest / len(shards))
        loudness = loudness * jnp.repeat(jnp.exp(heights), extent[dim] // blocks).reshape((-1,) + (1,) * (len(extent) - 1 - dim))
    return loudness


def split_up(count, total, most, slope):
    weights = [(1 << 20) // math.isqrt(standing ** slope) + 1 for standing in range(2, count + 1)]
    rest, given = total - most - (count - 1), [1] * (count - 1)
    while rest > 0:
        movable = [i for i in range(count - 1) if given[i] < most]
        pool, left = sum([weights[i] for i in movable]), rest
        for i in movable:
            more = min(most - given[i], max(1, left * weights[i] // pool), rest)
            given[i] = given[i] + more
            rest = rest - more
    return np.array([most] + given)


def uneven_parts(rng, number_of, total, bound, skew):
    if number_of == 2:
        one = jax.random.randint(rng, (), max(1, total - bound), min(bound, total - 1) + 1)
        return jnp.stack([one, total - one])
    sizes = jnp.asarray(split_up(number_of, total, bound, skew), jnp.int32)
    twos = (number_of - 1) // 2
    donor, taker = sizes[1:1 + 2 * twos:2], sizes[2:2 + 2 * twos:2]
    margin = jnp.minimum(donor - 1, bound - taker)
    passed = jax.random.randint(jax.random.fold_in(rng, 1), (twos,), 0, 1 << 20) % (margin + 1)
    sizes = sizes.at[1:1 + 2 * twos:2].set(donor - passed).at[2:2 + 2 * twos:2].set(taker + passed)
    return sizes[jax.random.permutation(jax.random.fold_in(rng, 2), number_of)]


def centred(own_key, dims, scale, most, shards=(), held_as=jnp.bfloat16):
    factor_of = shard_levels(own_key, dims, shards, -0.22, 0.18) if shards else 1.0
    values = jax.random.normal(own_key, dims, jnp.float32) * scale * factor_of
    return jnp.minimum(jnp.maximum(values, -most), most).astype(held_as)


def setup_inputs(seed: int = 0) -> dict:
    splits = jax.random.split(jax.random.key(seed), 22)
    tokens = centred(splits[0], (ROWS, L, D), 1.0, 6.0, ((0, 8),))
    lengths = uneven_parts(splits[1], ROWS, ROWS * L // 4, L, 2).astype(jnp.int32)
    groups = jax.vmap(lambda own: jnp.searchsorted(jnp.cumsum(uneven_parts(own, SEGS, L, L // 2, 1)), jnp.arange(L), side="right"))(jax.random.split(splits[2], ROWS)).reshape((ROWS, L)).astype(jnp.int32)
    key_mask = set_ends((jax.random.randint(splits[3], (ROWS, L), 0, 8) < 7).astype(jnp.int32), jax.random.fold_in(splits[3], 1), 0, 1)
    w_query = centred(splits[4], (D, H * DH), D ** -0.5, 0.21875, ((1, 4),))
    b_query = centred(splits[5], (H * DH,), 0.5, 3.0, ((0, 4),), jnp.float32)
    w_key = centred(splits[6], (D, H * DH), D ** -0.5, 0.21875, ((1, 4),))
    w_value = centred(splits[7], (D, H * DH), D ** -0.5, 0.21875, ((1, 4),))
    b_value = centred(splits[8], (H * DH,), 0.5, 3.0, ((0, 4),), jnp.float32)
    rel_bias = centred(splits[9], (H, NREL), 1.0, 4.0, ((0, 4),), jnp.float32)
    w_out = centred(splits[10], (H * DH, D), (D // 8) ** -0.5, 0.625, ((0, 4),))
    b_out = centred(splits[11], (D,), 0.5, 3.0, (), jnp.float32)
    gain_one = jnp.clip(1.0 + 0.15 * jax.random.normal(splits[12], (D,), jnp.float32), 0.25, 1.75)
    shift_one = centred(splits[13], (D,), 0.5, 3.0, (), jnp.float32)
    w_inner = centred(splits[14], (D, FF), D ** -0.5, 0.21875, ((1, 4),))
    b_inner = centred(splits[15], (FF,), 0.5, 3.0, ((0, 4),), jnp.float32)
    w_outer = centred(splits[16], (FF, D), FF ** -0.5, 0.109375, ((0, 4),))
    b_outer = centred(splits[17], (D,), 0.5, 3.0, (), jnp.float32)
    gain_two = jnp.clip(1.0 + 0.15 * jax.random.normal(splits[18], (D,), jnp.float32), 0.25, 1.75)
    shift_two = centred(splits[19], (D,), 0.5, 3.0, (), jnp.float32)
    cotangent = draw_cotangent(jax.random.fold_in(splits[21], 71), 0)
    return {"tokens": tokens, "lengths": lengths, "groups": groups, "key_mask": key_mask, "w_query": w_query, "b_query": b_query, "w_key": w_key, "w_value": w_value, "b_value": b_value, "rel_bias": rel_bias, "w_out": w_out, "b_out": b_out, "gain_one": gain_one, "shift_one": shift_one, "w_inner": w_inner, "b_inner": b_inner, "w_outer": w_outer, "b_outer": b_outer, "gain_two": gain_two, "shift_two": shift_two, "cotangent": cotangent}


@jax.custom_vjp
def low(v):
    return lax.optimization_barrier(v.astype(jnp.bfloat16)).astype(jnp.float32)

@jax.custom_vjp
def low_back(v):
    return v

def low_keep(v):
    return (low(v), None)

def low_pass(kept, grad):
    return (grad,)

def back_keep(v):
    return (v, None)

def back_low(kept, grad):
    return (low(grad),)
low.defvjp(low_keep, low_pass)
low_back.defvjp(back_keep, back_low)

def bucket_table(q_len, k_len, width):
    query = jnp.arange(q_len, dtype=jnp.int32)[:, None]
    keyed = jnp.arange(k_len, dtype=jnp.int32)[None, :]
    return (jnp.clip(keyed - 2 * query, -(width // 2), width // 2 - 1) + width // 2).astype(jnp.int32)

def allowed_keys(lengths, groups, key_mask):
    seq = groups.shape[1]
    keyed = jnp.arange(seq, dtype=jnp.int32)
    own = groups[:, 0::2]
    same = own[:, :, None] == groups[:, None, :]
    live = (keyed[None, :] < lengths[:, None]) & (key_mask == 1)
    self_key = keyed[None, :] == 2 * jnp.arange(seq // 2, dtype=jnp.int32)[:, None]
    return same & live[:, None, :] | self_key[None]

def matmul(left, right):
    return jnp.einsum('rld,de->rle', left, right, precision=lax.Precision.HIGHEST)

def norm_layer(value, gain, shift):
    centre = value - lax.optimization_barrier(jnp.mean(value, axis=-1, keepdims=True))
    spread = lax.optimization_barrier(jnp.mean(centre * centre, axis=-1, keepdims=True))
    return centre * lax.rsqrt(spread + 1e-05) * gain + shift

def reference(tokens, lengths, groups, key_mask, w_query, b_query, w_key, w_value, b_value, rel_bias, w_out, b_out, gain_one, shift_one, w_inner, b_inner, w_outer, b_outer, gain_two, shift_two, cotangent):
    allowed = allowed_keys(lengths, groups, key_mask)
    index = bucket_table(L // 2, L, NREL)

    def layer(wide, wq, bq, wk, wv, bv, rel, wo, bo, g1, s1, wi, bi, wt, bt, g2, s2):
        rows = wide.shape[0]
        pooled = lax.optimization_barrier(jnp.sum(wide.reshape(rows, L // 2, 2, D), axis=2)) * 0.5
        pooled_low = low(pooled)
        wide_low = low(wide)
        query = low(low_back(matmul(pooled_low, wq) + bq))
        keys = low(low_back(matmul(wide_low, wk)))
        values = low(low_back(matmul(wide_low, wv) + bv))
        bias = rel[:, index]

        def one_row(item):
            q_row, k_row, v_row, mask_row = item
            q_heads = q_row.reshape(L // 2, H, DH)
            k_heads = k_row.reshape(L, H, DH)
            v_heads = v_row.reshape(L, H, DH)
            raw = jnp.einsum('qhe,khe->hqk', q_heads, k_heads, precision=lax.Precision.HIGHEST) * 0.125 + bias
            raw = low_back(raw)
            masked = jnp.where(mask_row[None], raw, -1e+30)
            top = lax.optimization_barrier(jnp.max(masked, axis=-1, keepdims=True))
            expo = jnp.exp(masked - top)
            prob = expo / lax.optimization_barrier(jnp.sum(expo, axis=-1, keepdims=True))
            prob_low = low(prob)
            ctx = jnp.einsum('hqk,khe->qhe', prob_low, v_heads, precision=lax.Precision.HIGHEST)
            return ctx.reshape(L // 2, H * DH)
        context = lax.map(jax.checkpoint(one_row), (query, keys, values, allowed))
        context = low(low_back(context))
        attn = low_back(matmul(context, wo))
        first = pooled + (attn + bo)
        y_one = norm_layer(first, g1, s1)
        inner = low_back(matmul(low(y_one), wi) + bi)
        act = low(jax.nn.gelu(inner, approximate=False))
        ffn = low_back(matmul(act, wt))
        second = y_one + (ffn + bt)
        return norm_layer(second, g2, s2)
    floats = [item.astype(jnp.float32) for item in (tokens, w_query, b_query, w_key, w_value, b_value, rel_bias, w_out, b_out, gain_one, shift_one, w_inner, b_inner, w_outer, b_outer, gain_two, shift_two)]
    result, pull = jax.vjp(layer, *floats)
    grads = pull(cotangent.astype(jnp.float32))
    return (result.astype(jnp.bfloat16), grads[0].astype(jnp.bfloat16), grads[1], grads[2], grads[3], grads[4], grads[5], grads[6], grads[7], grads[8], grads[9], grads[10], grads[11], grads[12], grads[13], grads[14], grads[15], grads[16])
```

```python
import jax
import jax.numpy as jnp
from jax import lax
from jax.sharding import PartitionSpec as P


def diagonal_table(seq, width):
    span = 2 * seq
    offset = jnp.arange(span, dtype=jnp.int32)
    distance = jnp.where(offset < seq, offset, offset - span)
    bucket = jnp.clip(distance, -(width // 2), width // 2 - 1) + width // 2
    return (bucket[:, None] == jnp.arange(width, dtype=jnp.int32)[None, :]).astype(jnp.float32)


def skewed_bias(rel_bias, onehot, half, seq):
    heads = rel_bias.shape[0]
    span = 2 * seq
    line = jnp.dot(rel_bias, onehot.T, precision=lax.Precision.HIGHEST)
    tiled = jnp.tile(line, (1, half))[:, : half * (span - 2)]
    return tiled.reshape(heads, half, span - 2)[:, :, :seq]


def skewed_bias_grad(score_sum, onehot, half, seq):
    heads = score_sum.shape[0]
    span = 2 * seq
    padded = jnp.pad(score_sum, ((0, 0), (0, 0), (0, span - 2 - seq))).reshape(
        heads, half * (span - 2)
    )
    padded = jnp.pad(padded, ((0, 0), (0, 2 * half))).reshape(heads, half, span)
    along = jnp.sum(padded, axis=1)
    return jnp.dot(along, onehot, precision=lax.Precision.HIGHEST)


def allowed_keys(lengths, groups, key_mask):
    seq = groups.shape[1]
    keyed = jnp.arange(seq, dtype=jnp.int32)
    own = groups[:, 0::2]
    same = own[:, :, None] == groups[:, None, :]
    live = (keyed[None, :] < lengths[:, None]) & (key_mask == 1)
    self_key = keyed[None, :] == 2 * jnp.arange(seq // 2, dtype=jnp.int32)[:, None]
    return same & live[:, None, :] | self_key[None]


def norm_forward(value, gain, shift):
    centre = value - jnp.mean(value, axis=-1, keepdims=True)
    spread = jnp.mean(centre * centre, axis=-1, keepdims=True)
    factor = lax.rsqrt(spread + 1e-05)
    normed = centre * factor
    return (normed * gain + shift, normed, factor)


def norm_backward(grad_out, normed, factor, gain):
    grad_norm = grad_out * gain
    first_mean = jnp.mean(grad_norm, axis=-1, keepdims=True)
    second_mean = jnp.mean(grad_norm * normed, axis=-1, keepdims=True)
    grad_in = factor * (grad_norm - first_mean - normed * second_mean)
    return (grad_in, jnp.sum(grad_out * normed, axis=(0, 1)), jnp.sum(grad_out, axis=(0, 1)))


def project(left, right):
    return jnp.einsum("rld,de->rle", left, right, preferred_element_type=jnp.float32)


def project_back(left, right):
    return jnp.einsum("rle,de->rld", left, right, preferred_element_type=jnp.float32)


def weight_grad(left, right):
    return jnp.einsum("rld,rle->de", left, right, preferred_element_type=jnp.float32)


def exact_gelu(value):
    return jax.nn.gelu(value, approximate=False)


def swap_pairs(n, bit):
    return [(i, i ^ bit) for i in range(n)]


def half_of(a, which):
    size = a.shape[0] // 2
    return lax.dynamic_slice_in_dim(a, which * size, size, 0)


def in_order(mine, other, which):
    low = jnp.where(which == 0, mine, other)
    high = jnp.where(which == 0, other, mine)
    return jnp.concatenate([low, high], axis=0)


def tensor_sum(part):
    n = lax.axis_size("tensor")
    if n != 4:
        return lax.psum(part, "tensor")
    core = lax.axis_index("tensor") & 1
    got = lax.ppermute(half_of(part, 1 - core), "tensor", swap_pairs(n, 1))
    mine = half_of(part, core) + got
    mine = mine + lax.ppermute(mine, "tensor", swap_pairs(n, 2))
    other = lax.ppermute(mine, "tensor", swap_pairs(n, 1))
    return in_order(mine, other, core)


def rows_sum(part):
    return jnp.stack([tensor_sum(part[i]) for i in range(part.shape[0])])


INWARD = [(0, 2), (1, 3), (6, 4), (7, 5)]
MIDDLE = [(2, 4), (3, 5), (4, 2), (5, 3)]
OUTWARD = [(2, 0), (3, 1), (4, 6), (5, 7)]


def x_first(part):
    index = lax.axis_index("dp")
    x, z = index & 1, index >> 1
    centre = (z == 1) | (z == 2)
    got = lax.ppermute(half_of(part, 1 - x), "dp", swap_pairs(8, 1))
    mine = half_of(part, x) + got
    mine = mine + lax.ppermute(mine, "dp", INWARD)
    mine = mine + lax.ppermute(mine, "dp", MIDDLE)
    mine = jnp.where(centre, mine, lax.ppermute(mine, "dp", OUTWARD))
    other = lax.ppermute(mine, "dp", swap_pairs(8, 1))
    return in_order(mine, other, x)


def z_first(part):
    index = lax.axis_index("dp")
    z = index >> 1
    centre = (z == 1) | (z == 2)
    own = (z == 2).astype(jnp.int32)
    part = part + lax.ppermute(part, "dp", INWARD)
    got = lax.ppermute(half_of(part, 1 - own), "dp", MIDDLE)
    mine = half_of(part, own) + got
    mine = mine + lax.ppermute(mine, "dp", [(2, 3), (3, 2), (4, 5), (5, 4)])
    other = lax.ppermute(mine, "dp", MIDDLE)
    full = in_order(mine, other, own)
    return jnp.where(centre, full, lax.ppermute(full, "dp", OUTWARD))


def dp_sum(part, cut):
    if lax.axis_size("dp") != 8:
        return lax.psum(part, "dp")
    half = cut // 2
    return jnp.concatenate([x_first(part[:half]), x_first(part[half:cut]), z_first(part[cut:])], axis=0)


def local(
    tokens,
    lengths,
    groups,
    key_mask,
    w_query,
    b_query,
    w_key,
    w_value,
    b_value,
    rel_bias,
    w_out,
    b_out,
    gain_one,
    shift_one,
    w_inner,
    b_inner,
    w_outer,
    b_outer,
    gain_two,
    shift_two,
    cotangent,
):
    rows, seq, width = tokens.shape
    half = seq // 2
    heads, table = rel_bias.shape
    head_dim = w_query.shape[1] // heads
    wide = tokens.astype(jnp.float32)
    pooled = jnp.sum(wide.reshape(rows, half, 2, width), axis=2) * 0.5
    pooled_low = pooled.astype(jnp.bfloat16)
    query = (project(pooled_low, w_query) + b_query).astype(jnp.bfloat16)
    keys = project(tokens, w_key).astype(jnp.bfloat16)
    values = (project(tokens, w_value) + b_value).astype(jnp.bfloat16)
    query_heads = query.reshape(rows, half, heads, head_dim)
    key_heads = keys.reshape(rows, seq, heads, head_dim)
    value_heads = values.reshape(rows, seq, heads, head_dim)
    onehot = diagonal_table(seq, table)
    bias = skewed_bias(rel_bias, onehot, half, seq)
    allowed = allowed_keys(lengths, groups, key_mask)[:, None]

    def masked_scores():
        raw = (
            jnp.einsum(
                "rqhe,rkhe->rhqk", query_heads, key_heads, preferred_element_type=jnp.float32
            )
            * 0.125
            + bias[None]
        )
        return jnp.where(allowed, raw, -1e30)

    scores = masked_scores()
    top = jnp.max(scores, axis=-1, keepdims=True)
    expo = jnp.exp(scores - top)
    total = jnp.sum(expo, axis=-1, keepdims=True)
    log_total = top + jnp.log(total)
    prob_low = (expo / total).astype(jnp.bfloat16)
    context = jnp.einsum(
        "rhqk,rkhe->rqhe", prob_low, value_heads, preferred_element_type=jnp.float32
    )
    context = context.astype(jnp.bfloat16).reshape(rows, half, heads * head_dim)
    attn = rows_sum(project(context, w_out))
    first = pooled + (attn + b_out)
    y_one, normed_one, factor_one = norm_forward(first, gain_one, shift_one)
    y_low = y_one.astype(jnp.bfloat16)
    inner = project(y_low, w_inner) + b_inner
    act = exact_gelu(inner).astype(jnp.bfloat16)
    ffn = rows_sum(project(act, w_outer))
    second = y_one + (ffn + b_outer)
    result, normed_two, factor_two = norm_forward(second, gain_two, shift_two)
    output = result.astype(jnp.bfloat16)
    grad_out = cotangent.astype(jnp.float32)
    grad_second, grad_gain_two, grad_shift_two = norm_backward(
        grad_out, normed_two, factor_two, gain_two
    )
    grad_b_outer = jnp.sum(grad_second, axis=(0, 1))
    grad_ffn = grad_second.astype(jnp.bfloat16)
    grad_w_outer = weight_grad(act, grad_ffn)
    grad_act = project_back(grad_ffn, w_outer)
    gelu_pull = jax.vjp(exact_gelu, inner)[1]
    grad_inner = gelu_pull(grad_act)[0].astype(jnp.bfloat16)
    grad_b_inner = jnp.sum(grad_inner.astype(jnp.float32), axis=(0, 1))
    grad_w_inner = weight_grad(y_low, grad_inner)
    grad_y = grad_second + rows_sum(project_back(grad_inner, w_inner))
    grad_first, grad_gain_one, grad_shift_one = norm_backward(
        grad_y, normed_one, factor_one, gain_one
    )
    grad_b_out = jnp.sum(grad_first, axis=(0, 1))
    grad_attn = grad_first.astype(jnp.bfloat16)
    grad_w_out = weight_grad(context, grad_attn)
    grad_context = (
        project_back(grad_attn, w_out).astype(jnp.bfloat16).reshape(rows, half, heads, head_dim)
    )
    prob = jnp.exp(masked_scores() - log_total)
    grad_prob = jnp.einsum(
        "rqhe,rkhe->rhqk", grad_context, value_heads, preferred_element_type=jnp.float32
    )
    centre_term = jnp.sum(prob * grad_prob, axis=-1, keepdims=True)
    grad_scores = (prob * (grad_prob - centre_term)).astype(jnp.bfloat16)
    score_sum = jnp.sum(grad_scores.astype(jnp.float32), axis=0)
    grad_rel_bias = skewed_bias_grad(score_sum, onehot, half, seq)
    grad_query = (
        jnp.einsum("rhqk,rkhe->rqhe", grad_scores, key_heads, preferred_element_type=jnp.float32)
        * 0.125
    ).astype(jnp.bfloat16)
    grad_keys = (
        jnp.einsum("rhqk,rqhe->rkhe", grad_scores, query_heads, preferred_element_type=jnp.float32)
        * 0.125
    ).astype(jnp.bfloat16)
    grad_values = jnp.einsum(
        "rhqk,rqhe->rkhe", prob_low, grad_context, preferred_element_type=jnp.float32
    ).astype(jnp.bfloat16)
    grad_query = grad_query.reshape(rows, half, heads * head_dim)
    grad_keys = grad_keys.reshape(rows, seq, heads * head_dim)
    grad_values = grad_values.reshape(rows, seq, heads * head_dim)
    grad_b_query = jnp.sum(grad_query.astype(jnp.float32), axis=(0, 1))
    grad_b_value = jnp.sum(grad_values.astype(jnp.float32), axis=(0, 1))
    grad_w_query = weight_grad(pooled_low, grad_query)
    grad_w_key = weight_grad(tokens, grad_keys)
    grad_w_value = weight_grad(tokens, grad_values)
    pooled_part = project_back(grad_query, w_query)
    token_part = project_back(grad_keys, w_key) + project_back(grad_values, w_value)
    token_part = token_part + jnp.repeat(pooled_part * 0.5, 2, axis=1)
    token_sum = rows_sum(token_part)
    grad_tokens = (token_sum + jnp.repeat(grad_first * 0.5, 2, axis=1)).astype(jnp.bfloat16)
    small = jnp.concatenate(
        [
            grad_b_inner,
            grad_b_outer,
            grad_gain_two,
            grad_shift_two,
            grad_gain_one,
            grad_shift_one,
            grad_b_out,
            grad_rel_bias.reshape(-1),
            grad_b_query,
            grad_b_value,
        ]
    )
    small = jnp.pad(small, (0, 16 * width - small.shape[0])).reshape(16, width)
    grad_w_outer = dp_sum(grad_w_outer, 576)
    grad_w_inner = dp_sum(grad_w_inner, 576)
    e = heads * head_dim
    last = dp_sum(
        jnp.concatenate([grad_w_query.T, grad_w_key.T, grad_w_value.T, grad_w_out, small], axis=0), 576
    )
    grad_w_query, grad_w_key, grad_w_value = (last[i * e : (i + 1) * e].T for i in range(3))
    grad_w_out = last[3 * e : 4 * e]
    small = last[4 * e :].reshape(-1)
    (
        grad_b_inner,
        grad_b_outer,
        grad_gain_two,
        grad_shift_two,
        grad_gain_one,
        grad_shift_one,
        grad_b_out,
        grad_rel_bias,
    ) = (small[i * width : (i + 1) * width] for i in range(8))
    grad_rel_bias = grad_rel_bias.reshape(heads, table)
    grad_b_query = small[8 * width : 8 * width + e]
    grad_b_value = small[8 * width + e : 8 * width + 2 * e]
    return (
        output,
        grad_tokens,
        grad_w_query,
        grad_b_query,
        grad_w_key,
        grad_w_value,
        grad_b_value,
        grad_rel_bias,
        grad_w_out,
        grad_b_out,
        grad_gain_one,
        grad_shift_one,
        grad_w_inner,
        grad_b_inner,
        grad_w_outer,
        grad_b_outer,
        grad_gain_two,
        grad_shift_two,
    )


def solution(mesh):
    placed = (
        P("dp", None, None),
        P("dp"),
        P("dp", None),
        P("dp", None),
        P(None, "tensor"),
        P("tensor"),
        P(None, "tensor"),
        P(None, "tensor"),
        P("tensor"),
        P("tensor", None),
        P("tensor", None),
        P(),
        P(),
        P(),
        P(None, "tensor"),
        P("tensor"),
        P("tensor", None),
        P(),
        P(),
        P(),
        P("dp", None, None),
    )
    return jax.shard_map(
        local,
        mesh=mesh,
        in_specs=placed,
        out_specs=(
            P("dp", None, None),
            P("dp", None, None),
            P(None, "tensor"),
            P("tensor"),
            P(None, "tensor"),
            P(None, "tensor"),
            P("tensor"),
            P("tensor", None),
            P("tensor", None),
            P(),
            P(),
            P(),
            P(None, "tensor"),
            P("tensor"),
            P("tensor", None),
            P(),
            P(),
            P(),
        ),
        check_vma=False,
    )
```

```python
import functools

import jax
import jax.numpy as jnp
from jax import lax
from jax.experimental import pallas as pl
from jax.experimental.pallas import tpu as pltpu
from jax.sharding import PartitionSpec as P

F32 = jnp.float32
BF16 = jnp.bfloat16
VMEM_BYTES = 12 << 20
PIECE = 32

INWARD = [(0, 2), (1, 3), (6, 4), (7, 5)]
MIDDLE = [(2, 4), (3, 5), (4, 2), (5, 3)]
OUTWARD = [(2, 0), (3, 1), (4, 6), (5, 7)]
CENTRE_X = [(2, 3), (3, 2), (4, 5), (5, 4)]


def swap_pairs(n, bit):
    return [(i, i ^ bit) for i in range(n)]


def core_swap(a):
    return lax.ppermute(a, "tensor", swap_pairs(lax.axis_size("tensor"), 1))


def chip_swap(a):
    return lax.ppermute(a, "tensor", swap_pairs(lax.axis_size("tensor"), 2))


def x_swap(a):
    return lax.ppermute(a, "dp", swap_pairs(lax.axis_size("dp"), 1))


def hop(a, pairs):
    return lax.ppermute(a, "dp", pairs)


def on_line_of_four():
    return lax.axis_size("dp") == 8


def core_bit():
    return lax.axis_index("tensor") & 1


def x_bit():
    return lax.axis_index("dp") & 1


def centre_half():
    return ((lax.axis_index("dp") >> 1) >= 2).astype(jnp.int32)


def in_centre():
    z = lax.axis_index("dp") >> 1
    return (z == 1) | (z == 2)


def nn(a, b):
    return jnp.dot(a, b, preferred_element_type=F32)


def nt(a, b):
    return lax.dot_general(a, b, (((1,), (1,)), ((), ())), preferred_element_type=F32)


def tn(a, b):
    return lax.dot_general(a, b, (((0,), (0,)), ((), ())), preferred_element_type=F32)


def shape(dims, dtype=F32):
    return jax.ShapeDtypeStruct(dims, dtype)


ANY = pl.BlockSpec(memory_space=pl.ANY)
HBM = pl.BlockSpec(memory_space=pltpu.MemorySpace.HBM)
VMEM = pl.BlockSpec(memory_space=pltpu.VMEM)


class Late:
    def __init__(self, copy, ref):
        self.copy, self.ref, self.shape, self.here = copy, ref, ref.shape, False

    def __getitem__(self, at):
        if not self.here:
            self.copy.wait()
            self.here = True
        value = self.ref[at]
        return value.reshape(1, -1) if len(self.shape) == 1 and at is Ellipsis else value


def begin(token):
    pass


class Line:
    def __init__(self):
        self.token = pl.pallas_call(
            begin,
            out_specs=ANY,
            out_shape=shape((8, 128)),
            cost_estimate=pl.CostEstimate(flops=1 << 31, bytes_accessed=1 << 20, transcendentals=0),
        )()

    def __call__(self, body, outs, ins, late=(), scratch=(), left=(), onto=()):
        late = [item if isinstance(item, tuple) else (item, None) for item in late]
        far, near, given = len(late), len(ins), len(outs)

        def kernel(*refs):
            sources, plain, rest = refs[:far], refs[far : far + near], refs[far + near + 1 :]
            results, rest = rest[:given], rest[given + 1 :]
            if far:
                *spaces, sems = rest[len(rest) - far - 1 :]
                rest = rest[: len(rest) - far - 1]
                copies = [
                    pltpu.make_async_copy(src if pick is None else src.at[pick], space, sems.at[i])
                    for i, ((_, pick), src, space) in enumerate(zip(late, sources, spaces, strict=True))
                ]
                for copy in copies:
                    copy.start()
                sources = [Late(copy, space) for copy, space in zip(copies, spaces, strict=True)]
            body(*sources, *plain, *results, *rest)

        spaces = [
            pltpu.SMEM(a.shape, a.dtype) if a.size <= 8 else pltpu.VMEM(a.shape if pick is None else a.shape[1:], a.dtype)
            for a, pick in late
        ]
        result = pl.pallas_call(
            kernel,
            name=getattr(body, "func", body).__name__,
            in_specs=[HBM] * far + [ANY if i in onto else VMEM for i in range(near)] + [ANY],
            out_specs=[ANY if i in left else VMEM for i in range(given)] + [ANY],
            out_shape=[*outs, shape(self.token.shape)],
            scratch_shapes=[*scratch, *spaces, *([pltpu.SemaphoreType.DMA((far,))] if far else [])],
            input_output_aliases={far + i: o for i, o in zip(onto, left, strict=False)},
            compiler_params=pltpu.CompilerParams(vmem_limit_bytes=VMEM_BYTES),
            cost_estimate=pl.CostEstimate(flops=1024, bytes_accessed=1024, transcendentals=0),
        )(*(a for a, _ in late), *ins, self.token)
        self.token = result[-1]
        return result[:-1]


def hand_out(value, keep, send):
    size = keep.shape[0]
    for core in range(2):

        @pl.when(core_bit() == core)
        def _(core=core):
            keep[...] = value[core * size : (core + 1) * size]
            at = (1 - core) * size
            for ref in send:
                ref[...] = value[at : at + ref.shape[0]]
                at += ref.shape[0]


def chip_sum(keep, *refs):
    *got, out = refs
    size = got[0].shape[0]
    for i, ref in enumerate(got):
        at = slice(i * size, (i + 1) * size)
        out[at, :] = keep[at, :] + ref[...]


def total_sum(chip, far, *outs):
    size = outs[0].shape[0]
    for i, ref in enumerate(outs):
        at = slice(i * size, (i + 1) * size)
        ref[...] = chip[at, :] + far[at, :]


def gathered(parts, place):
    size, piece = place.shape[0] // 2, parts[0].shape[0]
    core = core_bit()
    for side, own in ((core, parts[: len(parts) // 2]), (1 - core, parts[len(parts) // 2 :])):
        for i, ref in enumerate(own):
            place[pl.ds(pl.multiple_of(side * size + i * piece, piece), piece), :] = ref[...]
    return place[...]


def head_lanes(size, heads, dim, h):
    lane = lax.broadcasted_iota(jnp.int32, (size, heads * dim), 1)
    return (lane >= h * dim) & (lane < (h + 1) * dim)


def attend(row, lens, tokens, groups, key_mask, wq, bq, wk, wv, bv, rel, wo, ctx, qo, ko, vo, prob, pooled_out, keep, *send):
    heads, table = rel.shape
    seq = tokens.shape[0]
    half = seq // 2
    dim = wq.shape[0] // heads
    tok = tokens[...]
    i = lax.broadcasted_iota(jnp.int32, (half, seq), 0)
    j = lax.broadcasted_iota(jnp.int32, (half, seq), 1)
    pick = jnp.where((j >> 1) == i, 0.5, 0.0).astype(BF16)
    pooled = nn(pick, tok)
    pooled_out[...] = pooled
    q = (nt(pooled.astype(BF16), wq[...]) + bq[...]).astype(BF16)
    k = nt(tok, wk[...]).astype(BF16)
    v = (nt(tok, wv[...]) + bv[...]).astype(BF16)
    qo[...] = q
    ko[...] = k
    vo[...] = v
    self_key = j == 2 * i
    group = groups[row : row + 1, :].astype(F32)
    place = lax.broadcasted_iota(jnp.int32, (1, seq), 1)
    live = (place < lens[row]) & (key_mask[row : row + 1, :] == 1)
    own = jnp.sum(jnp.where(self_key, group, 0.0), axis=1, keepdims=True)
    allowed = self_key | (own == jnp.where(live, group, -1.0))
    out = jnp.zeros((half, heads * dim), F32)
    for h in range(heads):
        span = 2 * seq
        wing = (span - table) // 2
        low = rel[h : h + 1, : table // 2]
        high = rel[h : h + 1, table // 2 :]
        line = jnp.concatenate(
            [
                high,
                jnp.broadcast_to(rel[h : h + 1, table - 1 :], (1, wing)),
                jnp.broadcast_to(rel[h : h + 1, :1], (1, wing)),
                low,
            ],
            axis=1,
        )
        bias = pltpu.roll(jnp.broadcast_to(line, (half, span)), 0, 1, stride=2, stride_axis=0)[:, :seq]
        raw = nt(jnp.where(head_lanes(half, heads, dim, h), q, 0), k) * 0.125 + bias
        score = jnp.where(allowed, raw, -1e30)
        expo = jnp.exp(score - jnp.max(score, axis=1, keepdims=True))
        p = expo * (1.0 / jnp.sum(expo, axis=1, keepdims=True))
        prob[h] = p
        out = out + nn(p.astype(BF16), jnp.where(head_lanes(seq, heads, dim, h), v, 0))
    low_out = out.astype(BF16)
    ctx[...] = low_out
    hand_out(nn(low_out, wo[...]), keep, send)


def normalise(value):
    centre = value - jnp.mean(value, axis=1, keepdims=True)
    factor = lax.rsqrt(jnp.mean(centre * centre, axis=1, keepdims=True) + 1e-05)
    return centre * factor, factor


def forward(count, b_out, gain, shift, wi, bi, wt, pooled, *refs):
    parts, refs = refs[:count], refs[count:]
    normed_o, factor_o, ylow_o, act_o, slope_o, keep, *send, place = refs
    first = pooled[...] + (gathered(parts, place) + b_out[...])
    normed, factor = normalise(first)
    normed_o[...] = normed
    factor_o[...] = factor
    y_low = (normed * gain[...] + shift[...]).astype(BF16)
    ylow_o[...] = y_low
    inner = nn(y_low, wi[...]) + bi[...]
    cdf = 0.5 + 0.5 * lax.erf(inner * 0.7071067811865476)
    slope_o[...] = cdf + inner * (0.3989422804014327 * jnp.exp(-0.5 * inner * inner))
    act = (inner * cdf).astype(BF16)
    act_o[...] = act
    hand_out(nn(act, wt[...]), keep, send)


def norm_back(grad, normed, factor, gain):
    scaled = grad * gain
    one = jnp.mean(scaled, axis=1, keepdims=True)
    two = jnp.mean(scaled * normed, axis=1, keepdims=True)
    return factor * (scaled - one - normed * two)


def over_rows(value):
    return jnp.sum(value, axis=0, keepdims=True)


def turn(row, count, gain_one, shift_one, b_outer, gain, shift, cot, wt, wi, normed_one, slope, *refs):
    parts, refs = refs[:count], refs[count + (row > 0) :]
    result, g_second_o, g_ffn_o, g_inner_o, small, keep, *send, place, low, done = refs
    y_one = normed_one[...] * gain_one[...] + shift_one[...]
    second = y_one + (gathered(parts, place) + b_outer[...])
    normed, factor = normalise(second)
    low[...] = (normed * gain[...] + shift[...]).astype(BF16)
    leave = pltpu.make_async_copy(low, result.at[row], done)
    leave.start()
    g_out = cot[...].astype(F32)
    g_second = norm_back(g_out, normed, factor, gain[...])
    g_second_o[...] = g_second
    g_ffn = g_second.astype(BF16)
    g_ffn_o[...] = g_ffn
    g_inner = (nt(g_ffn, wt[...]) * slope[...]).astype(BF16)
    g_inner_o[...] = g_inner
    hand_out(nt(g_inner, wi[...]), keep, send)
    small[0:1, :] = over_rows(g_inner.astype(F32))
    small[1:2, :] = over_rows(g_second)
    small[2:3, :] = over_rows(g_out * normed)
    small[3:4, :] = over_rows(g_out)
    leave.wait()


def ffn_weights(kind, lo, hi, act0, act1, g_ffn0, g_ffn1, y0, y1, g_in0, g_in1, *outs):
    def block(ref, lhs0, lhs1, rhs0, rhs1):
        ref[...] = tn(lhs0[:, lo:hi], rhs0[...]) + tn(lhs1[:, lo:hi], rhs1[...])

    outer = (act0, act1, g_ffn0, g_ffn1)
    inner = (y0, y1, g_in0, g_in1)
    if kind == "Z":
        block(outs[0].at[0], *outer)
        block(outs[0].at[1], *inner)
        return
    keep, send = outs

    @pl.when(x_bit() == 0)
    def _():
        block(keep, *outer)
        block(send, *inner)

    @pl.when(x_bit() != 0)
    def _():
        block(keep, *inner)
        block(send, *outer)


def attend_back(heads, count, gain, wo, wq, wk, wv, g_second, normed, factor, q_r, k_r, v_r, prob, *refs):
    parts, refs = refs[:count], refs[count:]
    g_first_o, g_attn_o, gs_o, gq_o, gk_o, gv_o, small, keep, *send, place = refs
    g_y = g_second[...] + gathered(parts, place)
    small[0:1, :] = over_rows(g_y * normed[...])
    small[1:2, :] = over_rows(g_y)
    g_first = norm_back(g_y, normed[...], factor[...], gain[...])
    g_first_o[...] = g_first
    small[2:3, :] = over_rows(g_first)
    g_attn = g_first.astype(BF16)
    g_attn_o[...] = g_attn
    g_ctx = nt(g_attn, wo[...]).astype(BF16)
    q, k, v = q_r[...], k_r[...], v_r[...]
    half, seq = q.shape[0], k.shape[0]
    dim = q.shape[1] // heads
    gq = jnp.zeros(q.shape, F32)
    gk = jnp.zeros(k.shape, F32)
    gv = jnp.zeros(k.shape, F32)
    for h in range(heads):
        own_q = head_lanes(half, heads, dim, h)
        own_k = head_lanes(seq, heads, dim, h)
        g_h = jnp.where(own_q, g_ctx, 0)
        p = prob[h]
        g_p = nt(g_h, v)
        g_s = (p * (g_p - jnp.sum(p * g_p, axis=1, keepdims=True))).astype(BF16)
        gs_o[h] = g_s
        gq = gq + nn(g_s, jnp.where(own_k, k, 0))
        gk = gk + tn(g_s, jnp.where(own_q, q, 0))
        gv = gv + tn(p.astype(BF16), g_h)
    gq = (gq * 0.125).astype(BF16)
    gk = (gk * 0.125).astype(BF16)
    gv = gv.astype(BF16)
    gq_o[...] = gq
    gk_o[...] = gk
    gv_o[...] = gv
    i = lax.broadcasted_iota(jnp.int32, (seq, half), 0)
    j = lax.broadcasted_iota(jnp.int32, (seq, half), 1)
    twice = jnp.where((i >> 1) == j, 0.5, 0.0).astype(BF16)
    gq_twice = nn(twice, gq).astype(BF16)
    hand_out(nn(gk, wk[...]) + nn(gv, wv[...]) + nn(gq_twice, wq[...]), keep, send)


def attn_weights_one(tokens, gq0, gq1, gv0, gv1, pooled0, pooled1, keep, send):
    def queries(ref):
        ref[...] = tn(gq0[...], pooled0[...].astype(BF16)) + tn(gq1[...], pooled1[...].astype(BF16))

    def values(ref):
        ref[...] = tn(gv0[...], tokens[0]) + tn(gv1[...], tokens[1])

    @pl.when(x_bit() == 0)
    def _():
        queries(keep)
        values(send)

    @pl.when(x_bit() != 0)
    def _():
        values(keep)
        queries(send)


def attn_weights_two(heads, table, tokens, gq0, gq1, gk0, gk1, gv0, gv1, ctx0, ctx1, ga0, ga1, gs0, gs1, t0, t1, a0, a1, keep, send):
    seq = tokens.shape[1]
    half, e = gq0.shape
    width = tokens.shape[2]
    i = lax.broadcasted_iota(jnp.int32, (half, half), 0)
    j = lax.broadcasted_iota(jnp.int32, (half, half), 1)
    flip = jnp.where(i + j == half - 1, 1.0, 0.0).astype(BF16)
    lane = lax.broadcasted_iota(jnp.int32, (1, table // 2), 1)
    span = 2 * seq
    pieces = []
    for h in range(heads):
        score = nn(flip, gs0[h]) + nn(flip, gs1[h])
        score = jnp.concatenate([score, jnp.zeros_like(score)], axis=1)
        along = over_rows(pltpu.roll(score, span - 2 * (half - 1), 1, stride=2, stride_axis=0))
        lo = jnp.sum(along[:, seq : span - table // 2], axis=1, keepdims=True)
        hi = jnp.sum(along[:, table // 2 : seq], axis=1, keepdims=True)
        pieces.append(along[:, span - table // 2 :] + jnp.where(lane == 0, lo, 0.0))
        pieces.append(along[:, : table // 2] + jnp.where(lane == table // 2 - 1, hi, 0.0))
    small = [t0[r : r + 1, :] + t1[r : r + 1, :] for r in range(4)]
    small += [a0[r : r + 1, :] + a1[r : r + 1, :] for r in range(3)]
    small.append(jnp.concatenate(pieces, axis=1))
    bq = over_rows(gq0[...].astype(F32)) + over_rows(gq1[...].astype(F32))
    bv = over_rows(gv0[...].astype(F32)) + over_rows(gv1[...].astype(F32))
    last = jnp.concatenate([bq, bv, jnp.zeros((1, width - 2 * e), F32)], axis=1)

    def keys(ref):
        ref[:e, :] = tn(gk0[...], tokens[0]) + tn(gk1[...], tokens[1])
        for r, value in enumerate(small):
            ref[e + r : e + r + 1, :] = value

    def outs(ref):
        ref[:e, :] = tn(ctx0[...], ga0[...]) + tn(ctx1[...], ga1[...])
        ref[e:, :] = jnp.broadcast_to(last, (ref.shape[0] - e, width))

    @pl.when(x_bit() == 0)
    def _():
        keys(keep)
        outs(send)

    @pl.when(x_bit() != 0)
    def _():
        outs(keep)
        keys(send)


def token_end(row, count, g_first, *refs):
    parts, refs = refs[:count], refs[count + (row > 0) :]
    result, place, twice, out, done = refs
    total = gathered(parts, place)
    half = g_first.shape[0]
    for s in range(g_first.shape[1] // 128):
        at = slice(s * 128, (s + 1) * 128)
        value = g_first[:, at] * 0.5
        twice[pl.ds(0, half, stride=2), :] = value
        twice[pl.ds(1, half, stride=2), :] = value
        out[:, at] = (total[:, at] + twice[...]).astype(BF16)
    leave = pltpu.make_async_copy(out, result.at[row], done)
    leave.start()
    leave.wait()


def add(a, b, out):
    out[...] = a[...] + b[...]


def add_split(a, b, keep, send):
    own = centre_half()
    keep[...] = a[own] + b[own]
    send[...] = a[1 - own] + b[1 - own]


def choose(mine, got, out):
    @pl.when(in_centre())
    def _():
        out[...] = mine[...]

    @pl.when(jnp.logical_not(in_centre()))
    def _():
        out[...] = got[...]


def ffn_end(kind, lo, count, *refs):
    parts, (outer, inner, *sems) = refs[:count], refs[-4:]

    def lay(which, low, high):
        @pl.when(which)
        def _():
            copies = [
                pltpu.make_async_copy(part, out.at[lo : lo + part.shape[0]], sem)
                for part, out, sem in zip((low, high), (outer, inner), sems, strict=True)
            ]
            for copy in copies:
                copy.start()
            for copy in copies:
                copy.wait()

    if kind == "X":
        lay(x_bit() == 0, parts[0], parts[1])
        lay(x_bit() != 0, parts[1], parts[0])
        return
    for here, one, two in ((in_centre(), *parts[:2]), (jnp.logical_not(in_centre()), *parts[2:])):
        lay(here & (centre_half() == 0), one, two)
        lay(here & (centre_half() == 1), two, one)


def attn_end_one(final, far, wq, wv):
    def lay(query, value):
        wq[...] = query[...]
        wv[...] = value[...]

    @pl.when(x_bit() == 0)
    def _():
        lay(final, far)

    @pl.when(x_bit() != 0)
    def _():
        lay(far, final)


def attn_end_two(final, far, wk, wo, bq, bv, rel, *small):
    e, width = wk.shape
    heads = rel.shape[0]
    table = width // heads

    def lay(one, two):
        wk[...] = one[:e, :]
        wo[...] = two[:e, :]
        for r, ref in enumerate(small):
            ref[...] = one[e + r, :]
        for h in range(heads):
            rel[h : h + 1, :] = one[e + len(small) : e + len(small) + 1, h * table : (h + 1) * table]
        bq[...] = two[e, :e]
        bv[...] = two[e, e : 2 * e]

    @pl.when(x_bit() == 0)
    def _():
        lay(final, far)

    @pl.when(x_bit() != 0)
    def _():
        lay(far, final)


CHUNKS = [("X", 0, 1), ("X", 1, 3), ("X", 3, 4), ("X", 4, 6)]


class TensorSum:
    def __init__(self, run, keep, *send):
        self.run, self.keep, self.got = run, keep, [core_swap(a) for a in send]

    def add(self):
        (self.chip,) = self.run(chip_sum, [shape(self.keep.shape)], [self.keep, *self.got])
        self.far = chip_swap(self.chip)

    def tot(self):
        mine = self.run(total_sum, [shape(a.shape) for a in self.got], [self.chip, self.far])
        self.parts = [*mine, *(core_swap(a) for a in mine)]


def others(a, bit):
    while bit < lax.axis_size("dp"):
        a = a + lax.ppermute(a, "dp", swap_pairs(lax.axis_size("dp"), bit))
        bit *= 2
    return a


class XFirst:
    def __init__(self, run, make):
        self.run, self.make_outs = run, make

    def plus(self, pairs):
        (self.mine,) = self.run(add, [shape(self.mine.shape)], [self.mine, self.got])
        self.got = hop(self.mine, pairs) if on_line_of_four() else None

    def make(self):
        self.mine, send = self.make_outs()
        self.got = x_swap(send)

    def xa(self):
        self.plus(INWARD)

    def ia(self):
        if on_line_of_four():
            self.plus(MIDDLE)

    def ma(self):
        if on_line_of_four():
            self.plus(OUTWARD)

    def ch(self):
        if on_line_of_four():
            (self.mine,) = self.run(choose, [shape(self.mine.shape)], [self.mine, self.got])
        else:
            self.mine = others(self.mine, 2)
        self.parts = [self.mine, x_swap(self.mine)]


class ZFirst:
    def __init__(self, run, make):
        self.run, self.make_outs = run, make

    def make(self):
        (self.whole,) = self.make_outs()
        self.got = hop(self.whole, INWARD) if on_line_of_four() else None

    def ia(self):
        if on_line_of_four():
            half = shape(self.whole.shape[1:])
            self.mine, send = self.run(add_split, [half, half], [self.whole, self.got])
            self.got = hop(send, MIDDLE)

    def ma(self):
        if on_line_of_four():
            (self.mine,) = self.run(add, [shape(self.mine.shape)], [self.mine, self.got])
            self.got = hop(self.mine, CENTRE_X)

    def xa(self):
        if on_line_of_four():
            (mine,) = self.run(add, [shape(self.mine.shape)], [self.mine, self.got])
            other = hop(mine, MIDDLE)
            self.parts = [mine, other, hop(mine, OUTWARD), hop(other, OUTWARD)]
        else:
            total, own = others(self.whole, 1), centre_half() == 0
            pair = [jnp.where(own, total[0], total[1]), jnp.where(own, total[1], total[0])]
            self.parts = pair + pair


def local(
    tokens,
    lengths,
    groups,
    key_mask,
    w_query,
    b_query,
    w_key,
    w_value,
    b_value,
    rel_bias,
    w_out,
    b_out,
    gain_one,
    shift_one,
    w_inner,
    b_inner,
    w_outer,
    b_outer,
    gain_two,
    shift_two,
    cotangent,
):
    rows, seq, width = tokens.shape
    half = seq // 2
    heads, table = rel_bias.shape
    e = w_query.shape[1]
    hidden = w_inner.shape[1]
    w_query, w_key, w_value = w_query.T, w_key.T, w_value.T
    run = Line()
    place = lambda n: pltpu.VMEM((n, width), F32)
    dma = pltpu.SemaphoreType.DMA

    def summands(n, piece=PIECE):
        return [shape((n // 2, width))] + [shape((piece, width))] * (n // 2 // piece)

    class Row:
        output = grad_tokens = None

        def __init__(self, r):
            self.r = r

        def attend(self):
            outs = [
                shape((half, e), BF16),
                shape((half, e), BF16),
                shape((seq, e), BF16),
                shape((seq, e), BF16),
                shape((heads, half, seq)),
                shape((half, width)),
            ]
            late = [lengths, (tokens, self.r), groups, key_mask]
            late += [w_query, b_query, w_key, w_value, b_value, rel_bias, w_out]
            got = run(functools.partial(attend, self.r), outs + summands(half), [], late=late)
            self.ctx, self.q, self.k, self.v, self.prob, self.pooled = got[:6]
            self.att = TensorSum(run, *got[6:])

        def forward(self):
            outs = [
                shape((half, width)),
                shape((half, 1)),
                shape((half, width), BF16),
                shape((half, hidden), BF16),
                shape((half, hidden)),
            ]
            parts = self.att.parts
            got = run(
                functools.partial(forward, len(parts)),
                outs + summands(half),
                [self.pooled, *parts],
                late=[b_out, gain_one, shift_one, w_inner, b_inner, w_outer],
                scratch=[place(half)],
            )
            self.normed, self.factor, self.y_low, self.act, self.slope = got[:5]
            self.ffn = TensorSum(run, *got[5:])

        def turn(self):
            outs = [
                shape((rows, half, width), BF16),
                shape((half, width)),
                shape((half, width), BF16),
                shape((half, hidden), BF16),
                shape((8, width)),
            ]
            parts = self.ffn.parts
            before = [] if Row.output is None else [Row.output]
            got = run(
                functools.partial(turn, self.r, len(parts)),
                outs + summands(half),
                [self.normed, self.slope, *parts, *before],
                late=[gain_one, shift_one, b_outer, gain_two, shift_two, (cotangent, self.r), w_outer, w_inner],
                scratch=[place(half), pltpu.VMEM((half, width), BF16), dma],
                left=(0,),
                onto=[2 + len(parts)] if before else (),
            )
            Row.output, self.g_second, self.g_ffn, self.g_inner, self.t_small = got[:5]
            self.back = TensorSum(run, *got[5:])

        def aback(self):
            outs = [
                shape((half, width)),
                shape((half, width), BF16),
                shape((heads, half, seq), BF16),
                shape((half, e), BF16),
                shape((seq, e), BF16),
                shape((seq, e), BF16),
                shape((8, width)),
            ]
            parts = self.back.parts
            got = run(
                functools.partial(attend_back, heads, len(parts)),
                outs + summands(seq, seq // 2),
                [self.g_second, self.normed, self.factor, self.q, self.k, self.v, self.prob, *parts],
                late=[gain_one, w_out, w_query, w_key, w_value],
                scratch=[place(half)],
            )
            self.g_first, self.g_attn, self.gs, self.gq, self.gk, self.gv, self.a_small = got[:7]
            self.tok = TensorSum(run, *got[7:])

        def tokend(self):
            parts = self.tok.parts
            before = [] if Row.grad_tokens is None else [Row.grad_tokens]
            (Row.grad_tokens,) = run(
                functools.partial(token_end, self.r, len(parts)),
                [shape((rows, seq, width), BF16)],
                [self.g_first, *parts, *before],
                scratch=[place(seq), pltpu.VMEM((seq, 128), F32), pltpu.VMEM((seq, width), BF16), dma],
                left=(0,),
                onto=[1 + len(parts)] if before else (),
            )

    r0, r1 = (Row(r) for r in range(rows))

    def ffn_chunk(kind, lo, hi):
        def make():
            outs = [shape((hi - lo, width))] * 2 if kind == "X" else [shape((2, hi - lo, width))]
            ins = [r0.act, r1.act, r0.g_ffn, r1.g_ffn, r0.y_low, r1.y_low, r0.g_inner, r1.g_inner]
            return run(functools.partial(ffn_weights, kind, lo, hi), outs, ins)

        return (XFirst if kind == "X" else ZFirst)(run, make)

    cuts = [(kind, lo * width // 6, hi * width // 6) for kind, lo, hi in CHUNKS]
    chunks = [ffn_chunk(*cut) for cut in cuts]
    x, z = ([chunk for chunk in chunks if isinstance(chunk, kind)] for kind in (XFirst, ZFirst))

    def attn_one():
        ins = [tokens, r0.gq, r1.gq, r0.gv, r1.gv, r0.pooled, r1.pooled]
        return run(attn_weights_one, [shape((e, width))] * 2, ins)

    def attn_two():
        ins = [tokens, r0.gq, r1.gq, r0.gk, r1.gk, r0.gv, r1.gv, r0.ctx, r1.ctx, r0.g_attn, r1.g_attn]
        ins += [r0.gs, r1.gs, r0.t_small, r1.t_small, r0.a_small, r1.a_small]
        return run(functools.partial(attn_weights_two, heads, table), [shape((e + 8, width))] * 2, ins)

    a = [XFirst(run, attn_one), XFirst(run, attn_two)]

    class Ffn:
        grads = ()

    def end(chunk):
        cut = cuts[chunks.index(chunk)]
        outs = [shape((hidden, width)), shape((width, hidden))]
        count = len(chunk.parts)
        Ffn.grads = run(
            functools.partial(ffn_end, *cut[:2], count),
            outs,
            [*chunk.parts, *Ffn.grads],
            scratch=[dma, dma],
            left=(0, 1),
            onto=[count, count + 1] if Ffn.grads else (),
        )

    def aend0():
        return run(attn_end_one, [shape((e, width))] * 2, a[0].parts)

    def aend1():
        outs = [shape((e, width))] * 2 + [shape((e,)), shape((e,)), shape((heads, table))] + [shape((width,))] * 7
        return run(attn_end_two, outs, a[1].parts)

    r0.attend()
    r0.att.add()
    r1.attend()
    r1.att.add()
    r0.att.tot()
    r0.forward()
    r1.att.tot()
    r0.ffn.add()
    r1.forward()
    r1.ffn.add()
    r0.ffn.tot()
    r0.turn()
    r1.ffn.tot()
    r0.back.add()
    r1.turn()
    x[3].make()
    x[0].make()
    r0.back.tot()
    r1.back.add()
    r0.aback()
    x[3].xa()
    r1.back.tot()
    x[1].make()
    r1.aback()
    a[0].make()
    x[0].xa()
    x[3].ia()
    x[1].xa()
    x[0].ia()
    x[3].ma()
    a[1].make()
    a[0].xa()
    x[1].ia()
    x[2].make()
    x[0].ma()
    r0.tok.add()
    x[3].ch()
    a[1].xa()
    a[0].ia()
    x[1].ma()
    x[2].xa()
    x[0].ch()
    a[0].ma()
    a[1].ia()
    end(x[3])
    x[1].ch()
    r0.tok.tot()
    r1.tok.add()
    x[2].ia()
    end(x[0])
    a[0].ch()
    a[1].ma()
    x[2].ma()
    end(x[1])
    r1.tok.tot()
    a[1].ch()
    grad_w_query, grad_w_value = aend0()
    x[2].ch()
    r0.tokend()
    grad_w_key, grad_w_out, grad_b_query, grad_b_value, grad_rel_bias, *small = aend1()
    r1.tokend()
    end(x[2])
    grad_w_outer, grad_w_inner = Ffn.grads
    grad_b_inner, grad_b_outer, grad_gain_two, grad_shift_two, grad_gain_one, grad_shift_one, grad_b_out = small
    return (
        Row.output,
        Row.grad_tokens,
        grad_w_query.T,
        grad_b_query,
        grad_w_key.T,
        grad_w_value.T,
        grad_b_value,
        grad_rel_bias,
        grad_w_out,
        grad_b_out,
        grad_gain_one,
        grad_shift_one,
        grad_w_inner,
        grad_b_inner,
        grad_w_outer,
        grad_b_outer,
        grad_gain_two,
        grad_shift_two,
    )


def solution(mesh):
    placed = (
        P("dp", None, None),
        P("dp"),
        P("dp", None),
        P("dp", None),
        P(None, "tensor"),
        P("tensor"),
        P(None, "tensor"),
        P(None, "tensor"),
        P("tensor"),
        P("tensor", None),
        P("tensor", None),
        P(),
        P(),
        P(),
        P(None, "tensor"),
        P("tensor"),
        P("tensor", None),
        P(),
        P(),
        P(),
        P("dp", None, None),
    )
    return jax.shard_map(
        local,
        mesh=mesh,
        in_specs=placed,
        out_specs=(
            P("dp", None, None),
            P("dp", None, None),
            P(None, "tensor"),
            P("tensor"),
            P(None, "tensor"),
            P(None, "tensor"),
            P("tensor"),
            P("tensor", None),
            P("tensor", None),
            P(),
            P(),
            P(),
            P(None, "tensor"),
            P("tensor"),
            P("tensor", None),
            P(),
            P(),
            P(),
        ),
        check_vma=False,
    )
```

```python
import functools

import jax
import jax.numpy as jnp
from jax import lax
from jax.experimental import pallas as pl
from jax.experimental.pallas import tpu as pltpu
from jax.sharding import PartitionSpec as P

F32 = jnp.float32
BF16 = jnp.bfloat16
VMEM_BYTES = 12 << 20
PIECE = 32

INWARD = [(0, 2), (1, 3), (6, 4), (7, 5)]
MIDDLE = [(2, 4), (3, 5), (4, 2), (5, 3)]
OUTWARD = [(2, 0), (3, 1), (4, 6), (5, 7)]
CENTRE_X = [(2, 3), (3, 2), (4, 5), (5, 4)]


def swap_pairs(n, bit):
    return [(i, i ^ bit) for i in range(n)]


def core_swap(a):
    return lax.ppermute(a, "tensor", swap_pairs(lax.axis_size("tensor"), 1))


def chip_swap(a):
    return lax.ppermute(a, "tensor", swap_pairs(lax.axis_size("tensor"), 2))


def x_swap(a):
    return lax.ppermute(a, "dp", swap_pairs(lax.axis_size("dp"), 1))


def hop(a, pairs):
    return lax.ppermute(a, "dp", pairs)


def on_line_of_four():
    return lax.axis_size("dp") == 8


def core_bit():
    return lax.axis_index("tensor") & 1


def x_bit():
    return lax.axis_index("dp") & 1


def centre_half():
    return ((lax.axis_index("dp") >> 1) >= 2).astype(jnp.int32)


def in_centre():
    z = lax.axis_index("dp") >> 1
    return (z == 1) | (z == 2)


def nn(a, b):
    return jnp.dot(a, b, preferred_element_type=F32)


def nt(a, b):
    return lax.dot_general(a, b, (((1,), (1,)), ((), ())), preferred_element_type=F32)


def tn(a, b):
    return lax.dot_general(a, b, (((0,), (0,)), ((), ())), preferred_element_type=F32)


def shape(dims, dtype=F32):
    return jax.ShapeDtypeStruct(dims, dtype)


ANY = pl.BlockSpec(memory_space=pl.ANY)
HBM = pl.BlockSpec(memory_space=pltpu.MemorySpace.HBM)
VMEM = pl.BlockSpec(memory_space=pltpu.VMEM)


class Late:
    def __init__(self, copy, ref):
        self.copy, self.ref, self.shape, self.here = copy, ref, ref.shape, False

    def __getitem__(self, at):
        if not self.here:
            self.copy.wait()
            self.here = True
        value = self.ref[at]
        return value.reshape(1, -1) if len(self.shape) == 1 and at is Ellipsis else value


def begin(token):
    pass


class Line:
    def __init__(self):
        self.token = pl.pallas_call(
            begin,
            out_specs=ANY,
            out_shape=shape((8, 128)),
            cost_estimate=pl.CostEstimate(flops=1 << 31, bytes_accessed=1 << 20, transcendentals=0),
        )()

    def __call__(self, body, outs, ins, late=(), scratch=(), left=(), onto=()):
        late = [item if isinstance(item, tuple) else (item, None) for item in late]
        far, near, given = len(late), len(ins), len(outs)

        def kernel(*refs):
            sources, plain, rest = refs[:far], refs[far : far + near], refs[far + near + 1 :]
            results, rest = rest[:given], rest[given + 1 :]
            if far:
                *spaces, sems = rest[len(rest) - far - 1 :]
                rest = rest[: len(rest) - far - 1]
                copies = [
                    pltpu.make_async_copy(src if pick is None else src.at[pick], space, sems.at[i])
                    for i, ((_, pick), src, space) in enumerate(zip(late, sources, spaces, strict=True))
                ]
                for copy in copies:
                    copy.start()
                sources = [Late(copy, space) for copy, space in zip(copies, spaces, strict=True)]
            body(*sources, *plain, *results, *rest)

        spaces = [
            pltpu.SMEM(a.shape, a.dtype) if a.size <= 8 else pltpu.VMEM(a.shape if pick is None else a.shape[1:], a.dtype)
            for a, pick in late
        ]
        result = pl.pallas_call(
            kernel,
            name=getattr(body, "func", body).__name__,
            in_specs=[HBM] * far + [ANY if i in onto else VMEM for i in range(near)] + [ANY],
            out_specs=[ANY if i in left else VMEM for i in range(given)] + [ANY],
            out_shape=[*outs, shape(self.token.shape)],
            scratch_shapes=[*scratch, *spaces, *([pltpu.SemaphoreType.DMA((far,))] if far else [])],
            input_output_aliases={far + i: o for i, o in zip(onto, left, strict=False)},
            compiler_params=pltpu.CompilerParams(vmem_limit_bytes=VMEM_BYTES),
            cost_estimate=pl.CostEstimate(flops=1024, bytes_accessed=1024, transcendentals=0),
        )(*(a for a, _ in late), *ins, self.token)
        self.token = result[-1]
        return result[:-1]


def hand_out(value, keep, send):
    size = keep.shape[0]
    for core in range(2):

        @pl.when(core_bit() == core)
        def _(core=core):
            keep[...] = value[core * size : (core + 1) * size]
            at = (1 - core) * size
            for ref in send:
                ref[...] = value[at : at + ref.shape[0]]
                at += ref.shape[0]


def chip_sum(keep, *refs):
    *got, out = refs
    size = got[0].shape[0]
    for i, ref in enumerate(got):
        at = slice(i * size, (i + 1) * size)
        out[at, :] = keep[at, :] + ref[...]


def total_sum(chip, far, *outs):
    size = outs[0].shape[0]
    for i, ref in enumerate(outs):
        at = slice(i * size, (i + 1) * size)
        ref[...] = chip[at, :] + far[at, :]


def gathered(parts, place):
    size, piece = place.shape[0] // 2, parts[0].shape[0]
    core = core_bit()
    for side, own in ((core, parts[: len(parts) // 2]), (1 - core, parts[len(parts) // 2 :])):
        for i, ref in enumerate(own):
            place[pl.ds(pl.multiple_of(side * size + i * piece, piece), piece), :] = ref[...]
    return place[...]


def head_lanes(size, heads, dim, h):
    lane = lax.broadcasted_iota(jnp.int32, (size, heads * dim), 1)
    return (lane >= h * dim) & (lane < (h + 1) * dim)


def attend(row, lens, tokens, groups, key_mask, wq, bq, wk, wv, bv, rel, wo, ctx, qo, ko, vo, prob, pooled_out, keep, *send):
    heads, table = rel.shape
    seq = tokens.shape[0]
    half = seq // 2
    dim = wq.shape[0] // heads
    tok = tokens[...]
    i = lax.broadcasted_iota(jnp.int32, (half, seq), 0)
    j = lax.broadcasted_iota(jnp.int32, (half, seq), 1)
    pick = jnp.where((j >> 1) == i, 0.5, 0.0).astype(BF16)
    pooled = nn(pick, tok)
    pooled_out[...] = pooled
    q = (nt(pooled.astype(BF16), wq[...]) + bq[...]).astype(BF16)
    k = nt(tok, wk[...]).astype(BF16)
    v = (nt(tok, wv[...]) + bv[...]).astype(BF16)
    qo[...] = q
    ko[...] = k
    vo[...] = v
    self_key = j == 2 * i
    group = groups[row : row + 1, :].astype(F32)
    place = lax.broadcasted_iota(jnp.int32, (1, seq), 1)
    live = (place < lens[row]) & (key_mask[row : row + 1, :] == 1)
    own = jnp.sum(jnp.where(self_key, group, 0.0), axis=1, keepdims=True)
    allowed = self_key | (own == jnp.where(live, group, -1.0))
    out = jnp.zeros((half, heads * dim), F32)
    for h in range(heads):
        span = 2 * seq
        wing = (span - table) // 2
        low = rel[h : h + 1, : table // 2]
        high = rel[h : h + 1, table // 2 :]
        line = jnp.concatenate(
            [
                high,
                jnp.broadcast_to(rel[h : h + 1, table - 1 :], (1, wing)),
                jnp.broadcast_to(rel[h : h + 1, :1], (1, wing)),
                low,
            ],
            axis=1,
        )
        bias = pltpu.roll(jnp.broadcast_to(line, (half, span)), 0, 1, stride=2, stride_axis=0)[:, :seq]
        raw = nt(jnp.where(head_lanes(half, heads, dim, h), q, 0), k) * 0.125 + bias
        score = jnp.where(allowed, raw, -1e30)
        expo = jnp.exp(score - jnp.max(score, axis=1, keepdims=True))
        p = expo * (1.0 / jnp.sum(expo, axis=1, keepdims=True))
        prob[h] = p
        out = out + nn(p.astype(BF16), jnp.where(head_lanes(seq, heads, dim, h), v, 0))
    low_out = out.astype(BF16)
    ctx[...] = low_out
    hand_out(nn(low_out, wo[...]), keep, send)


def normalise(value):
    centre = value - jnp.mean(value, axis=1, keepdims=True)
    factor = lax.rsqrt(jnp.mean(centre * centre, axis=1, keepdims=True) + 1e-05)
    return centre * factor, factor


def forward(count, b_out, gain, shift, wi, bi, wt, pooled, *refs):
    parts, refs = refs[:count], refs[count:]
    normed_o, factor_o, ylow_o, act_o, slope_o, keep, *send, place = refs
    first = pooled[...] + (gathered(parts, place) + b_out[...])
    normed, factor = normalise(first)
    normed_o[...] = normed
    factor_o[...] = factor
    y_low = (normed * gain[...] + shift[...]).astype(BF16)
    ylow_o[...] = y_low
    inner = nn(y_low, wi[...]) + bi[...]
    cdf = 0.5 + 0.5 * lax.erf(inner * 0.7071067811865476)
    slope_o[...] = cdf + inner * (0.3989422804014327 * jnp.exp(-0.5 * inner * inner))
    act = (inner * cdf).astype(BF16)
    act_o[...] = act
    hand_out(nn(act, wt[...]), keep, send)


def norm_back(grad, normed, factor, gain):
    scaled = grad * gain
    one = jnp.mean(scaled, axis=1, keepdims=True)
    two = jnp.mean(scaled * normed, axis=1, keepdims=True)
    return factor * (scaled - one - normed * two)


def over_rows(value):
    return jnp.sum(value, axis=0, keepdims=True)


def turn(row, count, again, gain_one, shift_one, b_outer, gain, shift, cot, wt, wi, normed_one, slope, *refs):
    parts, refs = refs[:count], refs[count + again :]
    result, g_second_o, g_ffn_o, g_inner_o, small, keep, *send, place, low, done = refs
    y_one = normed_one[...] * gain_one[...] + shift_one[...]
    second = y_one + (gathered(parts, place) + b_outer[...])
    normed, factor = normalise(second)
    low[...] = (normed * gain[...] + shift[...]).astype(BF16)
    leave = pltpu.make_async_copy(low, result.at[row], done)
    leave.start()
    g_out = cot[...].astype(F32)
    g_second = norm_back(g_out, normed, factor, gain[...])
    g_second_o[...] = g_second
    g_ffn = g_second.astype(BF16)
    g_ffn_o[...] = g_ffn
    g_inner = (nt(g_ffn, wt[...]) * slope[...]).astype(BF16)
    g_inner_o[...] = g_inner
    hand_out(nt(g_inner, wi[...]), keep, send)
    small[0:1, :] = over_rows(g_inner.astype(F32))
    small[1:2, :] = over_rows(g_second)
    small[2:3, :] = over_rows(g_out * normed)
    small[3:4, :] = over_rows(g_out)
    leave.wait()


def ffn_weights(kind, lo, hi, act0, act1, g_ffn0, g_ffn1, y0, y1, g_in0, g_in1, *outs):
    def block(ref, lhs0, lhs1, rhs0, rhs1):
        ref[...] = tn(lhs0[:, lo:hi], rhs0[...]) + tn(lhs1[:, lo:hi], rhs1[...])

    outer = (act0, act1, g_ffn0, g_ffn1)
    inner = (y0, y1, g_in0, g_in1)
    if kind == "Z":
        block(outs[0].at[0], *outer)
        block(outs[0].at[1], *inner)
        return
    keep, send = outs

    @pl.when(x_bit() == 0)
    def _():
        block(keep, *outer)
        block(send, *inner)

    @pl.when(x_bit() != 0)
    def _():
        block(keep, *inner)
        block(send, *outer)


def attend_back(heads, count, gain, wo, wq, wk, wv, g_second, normed, factor, q_r, k_r, v_r, prob, *refs):
    parts, refs = refs[:count], refs[count:]
    g_first_o, g_attn_o, gs_o, gq_o, gk_o, gv_o, small, keep, *send, place = refs
    g_y = g_second[...] + gathered(parts, place)
    small[0:1, :] = over_rows(g_y * normed[...])
    small[1:2, :] = over_rows(g_y)
    g_first = norm_back(g_y, normed[...], factor[...], gain[...])
    g_first_o[...] = g_first
    small[2:3, :] = over_rows(g_first)
    g_attn = g_first.astype(BF16)
    g_attn_o[...] = g_attn
    g_ctx = nt(g_attn, wo[...]).astype(BF16)
    q, k, v = q_r[...], k_r[...], v_r[...]
    half, seq = q.shape[0], k.shape[0]
    dim = q.shape[1] // heads
    gq = jnp.zeros(q.shape, F32)
    gk = jnp.zeros(k.shape, F32)
    gv = jnp.zeros(k.shape, F32)
    for h in range(heads):
        own_q = head_lanes(half, heads, dim, h)
        own_k = head_lanes(seq, heads, dim, h)
        g_h = jnp.where(own_q, g_ctx, 0)
        p = prob[h]
        g_p = nt(g_h, v)
        g_s = (p * (g_p - jnp.sum(p * g_p, axis=1, keepdims=True))).astype(BF16)
        gs_o[h] = g_s
        gq = gq + nn(g_s, jnp.where(own_k, k, 0))
        gk = gk + tn(g_s, jnp.where(own_q, q, 0))
        gv = gv + tn(p.astype(BF16), g_h)
    gq = (gq * 0.125).astype(BF16)
    gk = (gk * 0.125).astype(BF16)
    gv = gv.astype(BF16)
    gq_o[...] = gq
    gk_o[...] = gk
    gv_o[...] = gv
    i = lax.broadcasted_iota(jnp.int32, (seq, half), 0)
    j = lax.broadcasted_iota(jnp.int32, (seq, half), 1)
    twice = jnp.where((i >> 1) == j, 0.5, 0.0).astype(BF16)
    gq_twice = nn(twice, gq).astype(BF16)
    hand_out(nn(gk, wk[...]) + nn(gv, wv[...]) + nn(gq_twice, wq[...]), keep, send)


def attn_weights_one(tokens, gq0, gq1, gv0, gv1, pooled0, pooled1, keep, send):
    def queries(ref):
        ref[...] = tn(gq0[...], pooled0[...].astype(BF16)) + tn(gq1[...], pooled1[...].astype(BF16))

    def values(ref):
        ref[...] = tn(gv0[...], tokens[0]) + tn(gv1[...], tokens[1])

    @pl.when(x_bit() == 0)
    def _():
        queries(keep)
        values(send)

    @pl.when(x_bit() != 0)
    def _():
        values(keep)
        queries(send)


def attn_weights_two(heads, table, tokens, gq0, gq1, gk0, gk1, gv0, gv1, ctx0, ctx1, ga0, ga1, gs0, gs1, t0, t1, a0, a1, keep, send):
    seq = tokens.shape[1]
    half, e = gq0.shape
    width = tokens.shape[2]
    i = lax.broadcasted_iota(jnp.int32, (half, half), 0)
    j = lax.broadcasted_iota(jnp.int32, (half, half), 1)
    flip = jnp.where(i + j == half - 1, 1.0, 0.0).astype(BF16)
    lane = lax.broadcasted_iota(jnp.int32, (1, table // 2), 1)
    span = 2 * seq
    pieces = []
    for h in range(heads):
        score = nn(flip, gs0[h]) + nn(flip, gs1[h])
        score = jnp.concatenate([score, jnp.zeros_like(score)], axis=1)
        along = over_rows(pltpu.roll(score, span - 2 * (half - 1), 1, stride=2, stride_axis=0))
        lo = jnp.sum(along[:, seq : span - table // 2], axis=1, keepdims=True)
        hi = jnp.sum(along[:, table // 2 : seq], axis=1, keepdims=True)
        pieces.append(along[:, span - table // 2 :] + jnp.where(lane == 0, lo, 0.0))
        pieces.append(along[:, : table // 2] + jnp.where(lane == table // 2 - 1, hi, 0.0))
    small = [t0[r : r + 1, :] + t1[r : r + 1, :] for r in range(4)]
    small += [a0[r : r + 1, :] + a1[r : r + 1, :] for r in range(3)]
    small.append(jnp.concatenate(pieces, axis=1))
    bq = over_rows(gq0[...].astype(F32)) + over_rows(gq1[...].astype(F32))
    bv = over_rows(gv0[...].astype(F32)) + over_rows(gv1[...].astype(F32))
    last = jnp.concatenate([bq, bv, jnp.zeros((1, width - 2 * e), F32)], axis=1)

    def keys(ref):
        ref[:e, :] = tn(gk0[...], tokens[0]) + tn(gk1[...], tokens[1])
        for r, value in enumerate(small):
            ref[e + r : e + r + 1, :] = value

    def outs(ref):
        ref[:e, :] = tn(ctx0[...], ga0[...]) + tn(ctx1[...], ga1[...])
        ref[e:, :] = jnp.broadcast_to(last, (ref.shape[0] - e, width))

    @pl.when(x_bit() == 0)
    def _():
        keys(keep)
        outs(send)

    @pl.when(x_bit() != 0)
    def _():
        outs(keep)
        keys(send)


def token_end(row, count, again, g_first, *refs):
    parts, refs = refs[:count], refs[count + again :]
    result, place, twice, out, done = refs
    total = gathered(parts, place)
    half = g_first.shape[0]
    for s in range(g_first.shape[1] // 128):
        at = slice(s * 128, (s + 1) * 128)
        value = g_first[:, at] * 0.5
        twice[pl.ds(0, half, stride=2), :] = value
        twice[pl.ds(1, half, stride=2), :] = value
        out[:, at] = (total[:, at] + twice[...]).astype(BF16)
    leave = pltpu.make_async_copy(out, result.at[row], done)
    leave.start()
    leave.wait()


def add(a, b, out):
    out[...] = a[...] + b[...]


def add_split(a, b, keep, send):
    own = centre_half()
    keep[...] = a[own] + b[own]
    send[...] = a[1 - own] + b[1 - own]


def choose(mine, got, out):
    @pl.when(in_centre())
    def _():
        out[...] = mine[...]

    @pl.when(jnp.logical_not(in_centre()))
    def _():
        out[...] = got[...]


def ffn_end(kind, lo, count, *refs):
    parts, (outer, inner, *sems) = refs[:count], refs[-4:]

    def lay(which, low, high):
        @pl.when(which)
        def _():
            copies = [
                pltpu.make_async_copy(part, out.at[lo : lo + part.shape[0]], sem)
                for part, out, sem in zip((low, high), (outer, inner), sems, strict=True)
            ]
            for copy in copies:
                copy.start()
            for copy in copies:
                copy.wait()

    if kind == "X":
        lay(x_bit() == 0, parts[0], parts[1])
        lay(x_bit() != 0, parts[1], parts[0])
        return
    for here, one, two in ((in_centre(), *parts[:2]), (jnp.logical_not(in_centre()), *parts[2:])):
        lay(here & (centre_half() == 0), one, two)
        lay(here & (centre_half() == 1), two, one)


def attn_end_one(final, far, wq, wv):
    def lay(query, value):
        wq[...] = query[...]
        wv[...] = value[...]

    @pl.when(x_bit() == 0)
    def _():
        lay(final, far)

    @pl.when(x_bit() != 0)
    def _():
        lay(far, final)


def attn_end_two(final, far, wk, wo, bq, bv, rel, *small):
    e, width = wk.shape
    heads = rel.shape[0]
    table = width // heads

    def lay(one, two):
        wk[...] = one[:e, :]
        wo[...] = two[:e, :]
        for r, ref in enumerate(small):
            ref[...] = one[e + r, :]
        for h in range(heads):
            rel[h : h + 1, :] = one[e + len(small) : e + len(small) + 1, h * table : (h + 1) * table]
        bq[...] = two[e, :e]
        bv[...] = two[e, e : 2 * e]

    @pl.when(x_bit() == 0)
    def _():
        lay(final, far)

    @pl.when(x_bit() != 0)
    def _():
        lay(far, final)


CHUNKS = [("X", 0, 2), ("X", 2, 4), ("X", 4, 5), ("Z", 5, 6)]


class TensorSum:
    def __init__(self, run, keep, *send):
        self.run, self.keep, self.got = run, keep, [core_swap(a) for a in send]

    def add(self):
        (self.chip,) = self.run(chip_sum, [shape(self.keep.shape)], [self.keep, *self.got])
        self.far = chip_swap(self.chip)

    def tot(self):
        mine = self.run(total_sum, [shape(a.shape) for a in self.got], [self.chip, self.far])
        self.parts = [*mine, *(core_swap(a) for a in mine)]


def others(a, bit):
    while bit < lax.axis_size("dp"):
        a = a + lax.ppermute(a, "dp", swap_pairs(lax.axis_size("dp"), bit))
        bit *= 2
    return a


class XFirst:
    def __init__(self, run, make):
        self.run, self.make_outs = run, make

    def plus(self, pairs):
        (self.mine,) = self.run(add, [shape(self.mine.shape)], [self.mine, self.got])
        self.got = hop(self.mine, pairs) if on_line_of_four() else None

    def make(self):
        self.mine, send = self.make_outs()
        self.got = x_swap(send)

    def xa(self):
        self.plus(INWARD)

    def ia(self):
        if on_line_of_four():
            self.plus(MIDDLE)

    def ma(self):
        if on_line_of_four():
            self.plus(OUTWARD)

    def ch(self):
        if on_line_of_four():
            (self.mine,) = self.run(choose, [shape(self.mine.shape)], [self.mine, self.got])
        else:
            self.mine = others(self.mine, 2)
        self.parts = [self.mine, x_swap(self.mine)]


class ZFirst:
    def __init__(self, run, make):
        self.run, self.make_outs = run, make

    def make(self):
        (self.whole,) = self.make_outs()
        self.got = hop(self.whole, INWARD) if on_line_of_four() else None

    def ia(self):
        if on_line_of_four():
            half = shape(self.whole.shape[1:])
            self.mine, send = self.run(add_split, [half, half], [self.whole, self.got])
            self.got = hop(send, MIDDLE)

    def ma(self):
        if on_line_of_four():
            (self.mine,) = self.run(add, [shape(self.mine.shape)], [self.mine, self.got])
            self.got = hop(self.mine, CENTRE_X)

    def xa(self):
        if on_line_of_four():
            (mine,) = self.run(add, [shape(self.mine.shape)], [self.mine, self.got])
            other = hop(mine, MIDDLE)
            self.parts = [mine, other, hop(mine, OUTWARD), hop(other, OUTWARD)]
        else:
            total, own = others(self.whole, 1), centre_half() == 0
            pair = [jnp.where(own, total[0], total[1]), jnp.where(own, total[1], total[0])]
            self.parts = pair + pair


def local(
    tokens,
    lengths,
    groups,
    key_mask,
    w_query,
    b_query,
    w_key,
    w_value,
    b_value,
    rel_bias,
    w_out,
    b_out,
    gain_one,
    shift_one,
    w_inner,
    b_inner,
    w_outer,
    b_outer,
    gain_two,
    shift_two,
    cotangent,
):
    rows, seq, width = tokens.shape
    half = seq // 2
    heads, table = rel_bias.shape
    e = w_query.shape[1]
    hidden = w_inner.shape[1]
    w_query, w_key, w_value = w_query.T, w_key.T, w_value.T
    run = Line()
    place = lambda n: pltpu.VMEM((n, width), F32)
    dma = pltpu.SemaphoreType.DMA

    def summands(n, piece=PIECE):
        return [shape((n // 2, width))] + [shape((piece, width))] * (n // 2 // piece)

    class Row:
        output = grad_tokens = None

        def __init__(self, r):
            self.r = r

        def attend(self):
            outs = [
                shape((half, e), BF16),
                shape((half, e), BF16),
                shape((seq, e), BF16),
                shape((seq, e), BF16),
                shape((heads, half, seq)),
                shape((half, width)),
            ]
            late = [lengths, (tokens, self.r), groups, key_mask]
            late += [w_query, b_query, w_key, w_value, b_value, rel_bias, w_out]
            got = run(functools.partial(attend, self.r), outs + summands(half), [], late=late)
            self.ctx, self.q, self.k, self.v, self.prob, self.pooled = got[:6]
            self.att = TensorSum(run, *got[6:])

        def forward(self):
            outs = [
                shape((half, width)),
                shape((half, 1)),
                shape((half, width), BF16),
                shape((half, hidden), BF16),
                shape((half, hidden)),
            ]
            parts = self.att.parts
            got = run(
                functools.partial(forward, len(parts)),
                outs + summands(half),
                [self.pooled, *parts],
                late=[b_out, gain_one, shift_one, w_inner, b_inner, w_outer],
                scratch=[place(half)],
            )
            self.normed, self.factor, self.y_low, self.act, self.slope = got[:5]
            self.ffn = TensorSum(run, *got[5:])

        def turn(self):
            outs = [
                shape((rows, half, width), BF16),
                shape((half, width)),
                shape((half, width), BF16),
                shape((half, hidden), BF16),
                shape((8, width)),
            ]
            parts = self.ffn.parts
            before = [] if Row.output is None else [Row.output]
            got = run(
                functools.partial(turn, self.r, len(parts), len(before)),
                outs + summands(half),
                [self.normed, self.slope, *parts, *before],
                late=[gain_one, shift_one, b_outer, gain_two, shift_two, (cotangent, self.r), w_outer, w_inner],
                scratch=[place(half), pltpu.VMEM((half, width), BF16), dma],
                left=(0,),
                onto=[2 + len(parts)] if before else (),
            )
            Row.output, self.g_second, self.g_ffn, self.g_inner, self.t_small = got[:5]
            self.back = TensorSum(run, *got[5:])

        def aback(self):
            outs = [
                shape((half, width)),
                shape((half, width), BF16),
                shape((heads, half, seq), BF16),
                shape((half, e), BF16),
                shape((seq, e), BF16),
                shape((seq, e), BF16),
                shape((8, width)),
            ]
            parts = self.back.parts
            got = run(
                functools.partial(attend_back, heads, len(parts)),
                outs + summands(seq, seq // 2),
                [self.g_second, self.normed, self.factor, self.q, self.k, self.v, self.prob, *parts],
                late=[gain_one, w_out, w_query, w_key, w_value],
                scratch=[place(half)],
            )
            self.g_first, self.g_attn, self.gs, self.gq, self.gk, self.gv, self.a_small = got[:7]
            self.tok = TensorSum(run, *got[7:])

        def tokend(self):
            parts = self.tok.parts
            before = [] if Row.grad_tokens is None else [Row.grad_tokens]
            (Row.grad_tokens,) = run(
                functools.partial(token_end, self.r, len(parts), len(before)),
                [shape((rows, seq, width), BF16)],
                [self.g_first, *parts, *before],
                scratch=[place(seq), pltpu.VMEM((seq, 128), F32), pltpu.VMEM((seq, width), BF16), dma],
                left=(0,),
                onto=[1 + len(parts)] if before else (),
            )

    r0, r1 = (Row(r) for r in range(rows))

    def ffn_chunk(kind, lo, hi):
        def make():
            outs = [shape((hi - lo, width))] * 2 if kind == "X" else [shape((2, hi - lo, width))]
            ins = [r0.act, r1.act, r0.g_ffn, r1.g_ffn, r0.y_low, r1.y_low, r0.g_inner, r1.g_inner]
            return run(functools.partial(ffn_weights, kind, lo, hi), outs, ins)

        return (XFirst if kind == "X" else ZFirst)(run, make)

    cuts = [(kind, lo * width // 6, hi * width // 6) for kind, lo, hi in CHUNKS]
    chunks = [ffn_chunk(*cut) for cut in cuts]
    x, z = ([chunk for chunk in chunks if isinstance(chunk, kind)] for kind in (XFirst, ZFirst))

    def attn_one():
        ins = [tokens, r0.gq, r1.gq, r0.gv, r1.gv, r0.pooled, r1.pooled]
        return run(attn_weights_one, [shape((e, width))] * 2, ins)

    def attn_two():
        ins = [tokens, r0.gq, r1.gq, r0.gk, r1.gk, r0.gv, r1.gv, r0.ctx, r1.ctx, r0.g_attn, r1.g_attn]
        ins += [r0.gs, r1.gs, r0.t_small, r1.t_small, r0.a_small, r1.a_small]
        return run(functools.partial(attn_weights_two, heads, table), [shape((e + 8, width))] * 2, ins)

    a = [XFirst(run, attn_one), XFirst(run, attn_two)]

    class Ffn:
        grads = ()

    def end(chunk):
        cut = cuts[chunks.index(chunk)]
        outs = [shape((hidden, width)), shape((width, hidden))]
        count = len(chunk.parts)
        Ffn.grads = run(
            functools.partial(ffn_end, *cut[:2], count),
            outs,
            [*chunk.parts, *Ffn.grads],
            scratch=[dma, dma],
            left=(0, 1),
            onto=[count, count + 1] if Ffn.grads else (),
        )

    def aend0():
        return run(attn_end_one, [shape((e, width))] * 2, a[0].parts)

    def aend1():
        outs = [shape((e, width))] * 2 + [shape((e,)), shape((e,)), shape((heads, table))] + [shape((width,))] * 7
        return run(attn_end_two, outs, a[1].parts)

    r0.attend()
    r0.att.add()
    r1.attend()
    r1.att.add()
    r0.att.tot()
    r0.forward()
    r0.ffn.add()
    r1.att.tot()
    r1.forward()
    r1.ffn.add()
    r0.ffn.tot()
    r0.turn()
    r1.ffn.tot()
    r0.back.add()
    r1.turn()
    z[0].make()
    x[1].make()
    r1.back.add()
    r0.back.tot()
    r0.aback()
    x[2].make()
    x[0].make()
    r1.back.tot()
    r1.aback()
    x[1].xa()
    z[0].ia()
    a[1].make()
    a[0].make()
    z[0].ma()
    x[0].xa()
    x[1].ia()
    r1.tok.add()
    a[0].xa()
    r0.tok.add()
    x[0].ia()
    x[1].ma()
    r1.tok.tot()
    a[1].xa()
    a[0].ia()
    x[2].xa()
    x[0].ma()
    x[1].ch()
    z[0].xa()
    a[0].ma()
    a[1].ia()
    x[0].ch()
    r0.tok.tot()
    end(x[1])
    a[1].ma()
    a[0].ch()
    x[2].ia()
    end(x[0])
    r1.tokend()
    a[1].ch()
    x[2].ma()
    x[2].ch()
    grad_w_query, grad_w_value = aend0()
    r0.tokend()
    grad_w_key, grad_w_out, grad_b_query, grad_b_value, grad_rel_bias, *small = aend1()
    end(z[0])
    end(x[2])
    grad_w_outer, grad_w_inner = Ffn.grads
    grad_b_inner, grad_b_outer, grad_gain_two, grad_shift_two, grad_gain_one, grad_shift_one, grad_b_out = small
    return (
        Row.output,
        Row.grad_tokens,
        grad_w_query.T,
        grad_b_query,
        grad_w_key.T,
        grad_w_value.T,
        grad_b_value,
        grad_rel_bias,
        grad_w_out,
        grad_b_out,
        grad_gain_one,
        grad_shift_one,
        grad_w_inner,
        grad_b_inner,
        grad_w_outer,
        grad_b_outer,
        grad_gain_two,
        grad_shift_two,
    )


def solution(mesh):
    placed = (
        P("dp", None, None),
        P("dp"),
        P("dp", None),
        P("dp", None),
        P(None, "tensor"),
        P("tensor"),
        P(None, "tensor"),
        P(None, "tensor"),
        P("tensor"),
        P("tensor", None),
        P("tensor", None),
        P(),
        P(),
        P(),
        P(None, "tensor"),
        P("tensor"),
        P("tensor", None),
        P(),
        P(),
        P(),
        P("dp", None, None),
    )
    return jax.shard_map(
        local,
        mesh=mesh,
        in_specs=placed,
        out_specs=(
            P("dp", None, None),
            P("dp", None, None),
            P(None, "tensor"),
            P("tensor"),
            P(None, "tensor"),
            P(None, "tensor"),
            P("tensor"),
            P("tensor", None),
            P("tensor", None),
            P(),
            P(),
            P(),
            P(None, "tensor"),
            P("tensor"),
            P("tensor", None),
            P(),
            P(),
            P(),
        ),
        check_vma=False,
    )
```

```python
import functools

import jax
import jax.numpy as jnp
from jax import lax
from jax.experimental import pallas as pl
from jax.experimental.pallas import tpu as pltpu
from jax.sharding import PartitionSpec as P

F32 = jnp.float32
BF16 = jnp.bfloat16
VMEM_BYTES = 12 << 20
PIECE = 32

INWARD = [(0, 2), (1, 3), (6, 4), (7, 5)]
MIDDLE = [(2, 4), (3, 5), (4, 2), (5, 3)]
OUTWARD = [(2, 0), (3, 1), (4, 6), (5, 7)]
CENTRE_X = [(2, 3), (3, 2), (4, 5), (5, 4)]


def swap_pairs(n, bit):
    return [(i, i ^ bit) for i in range(n)]


def core_swap(a):
    return lax.ppermute(a, "tensor", swap_pairs(lax.axis_size("tensor"), 1))


def chip_swap(a):
    return lax.ppermute(a, "tensor", swap_pairs(lax.axis_size("tensor"), 2))


def x_swap(a):
    return lax.ppermute(a, "dp", swap_pairs(lax.axis_size("dp"), 1))


def hop(a, pairs):
    return lax.ppermute(a, "dp", pairs)


def on_line_of_four():
    return lax.axis_size("dp") == 8


def core_bit():
    return lax.axis_index("tensor") & 1


def x_bit():
    return lax.axis_index("dp") & 1


def centre_half():
    return ((lax.axis_index("dp") >> 1) >= 2).astype(jnp.int32)


def in_centre():
    z = lax.axis_index("dp") >> 1
    return (z == 1) | (z == 2)


def nn(a, b):
    return jnp.dot(a, b, preferred_element_type=F32)


def nt(a, b):
    return lax.dot_general(a, b, (((1,), (1,)), ((), ())), preferred_element_type=F32)


def tn(a, b):
    return lax.dot_general(a, b, (((0,), (0,)), ((), ())), preferred_element_type=F32)


def shape(dims, dtype=F32):
    return jax.ShapeDtypeStruct(dims, dtype)


ANY = pl.BlockSpec(memory_space=pl.ANY)
VMEM = pl.BlockSpec(memory_space=pltpu.VMEM)


class View:
    def __init__(self, ref, pick):
        self.ref = ref if pick is None else ref.at[pick]
        self.shape = self.ref.shape

    def __getitem__(self, at):
        value = self.ref[at]
        return value.reshape(1, -1) if len(self.shape) == 1 and at is Ellipsis else value


def begin(token):
    token[...] = jnp.zeros_like(token)


class Line:
    def __init__(self):
        self.token = pl.pallas_call(
            begin,
            out_specs=VMEM,
            out_shape=shape((8, 128)),
            cost_estimate=pl.CostEstimate(flops=1 << 31, bytes_accessed=1 << 20, transcendentals=0),
        )()

    def __call__(self, body, outs, ins, late=(), scratch=(), left=(), onto=()):
        late = [item if isinstance(item, tuple) else (item, None) for item in late]
        far, near, given = len(late), len(ins), len(outs)

        def kernel(*refs):
            views = [View(ref, pick) for ref, (_, pick) in zip(refs, late, strict=False)]
            rest = refs[far + near + 1 :]
            body(*views, *refs[far : far + near], *rest[:given], *rest[given + 1 :])

        result = pl.pallas_call(
            kernel,
            name=getattr(body, "func", body).__name__,
            in_specs=[VMEM] * far
            + [ANY if i in onto else VMEM for i in range(near)]
            + [ANY],
            out_specs=[ANY if i in left else VMEM for i in range(given)] + [ANY],
            out_shape=[*outs, shape(self.token.shape)],
            scratch_shapes=list(scratch),
            input_output_aliases={far + i: o for i, o in zip(onto, left, strict=False)},
            compiler_params=pltpu.CompilerParams(vmem_limit_bytes=VMEM_BYTES),
            cost_estimate=pl.CostEstimate(flops=1024, bytes_accessed=1024, transcendentals=0),
        )(*(a for a, _ in late), *ins, self.token)
        self.token = result[-1]
        return result[:-1]


def hand_out(value, keep, send):
    size = keep.shape[0]
    for core in range(2):

        @pl.when(core_bit() == core)
        def _(core=core):
            keep[...] = value[core * size : (core + 1) * size]
            at = (1 - core) * size
            for ref in send:
                ref[...] = value[at : at + ref.shape[0]]
                at += ref.shape[0]


def chip_sum(keep, *refs):
    *got, out = refs
    size = got[0].shape[0]
    for i, ref in enumerate(got):
        at = slice(i * size, (i + 1) * size)
        out[at, :] = keep[at, :] + ref[...]


def total_sum(chip, far, *outs):
    size = outs[0].shape[0]
    for i, ref in enumerate(outs):
        at = slice(i * size, (i + 1) * size)
        ref[...] = chip[at, :] + far[at, :]


def gathered(parts, place):
    size, piece = place.shape[0] // 2, parts[0].shape[0]
    core = core_bit()
    for side, own in ((core, parts[: len(parts) // 2]), (1 - core, parts[len(parts) // 2 :])):
        for i, ref in enumerate(own):
            place[pl.ds(pl.multiple_of(side * size + i * piece, piece), piece), :] = ref[...]
    return place[...]


def head_lanes(size, heads, dim, h):
    lane = lax.broadcasted_iota(jnp.int32, (size, heads * dim), 1)
    return (lane >= h * dim) & (lane < (h + 1) * dim)


def attend(row, lens, tokens, groups, key_mask, wq, bq, wk, wv, bv, rel, wo, ctx, qo, ko, vo, prob, pooled_out, keep, *send):
    heads, table = rel.shape
    seq = tokens.shape[0]
    half = seq // 2
    dim = wq.shape[0] // heads
    tok = tokens[...]
    i = lax.broadcasted_iota(jnp.int32, (half, seq), 0)
    j = lax.broadcasted_iota(jnp.int32, (half, seq), 1)
    pick = jnp.where((j >> 1) == i, 0.5, 0.0).astype(BF16)
    pooled = nn(pick, tok)
    pooled_out[...] = pooled
    q = (nt(pooled.astype(BF16), wq[...]) + bq[...]).astype(BF16)
    k = nt(tok, wk[...]).astype(BF16)
    v = (nt(tok, wv[...]) + bv[...]).astype(BF16)
    qo[...] = q
    ko[...] = k
    vo[...] = v
    self_key = j == 2 * i
    group = groups[row : row + 1, :].astype(F32)
    place = lax.broadcasted_iota(jnp.int32, (1, seq), 1)
    live = (place < lens[...][:, row : row + 1]) & (key_mask[row : row + 1, :] == 1)
    own = jnp.sum(jnp.where(self_key, group, 0.0), axis=1, keepdims=True)
    allowed = self_key | (own == jnp.where(live, group, -1.0))
    out = jnp.zeros((half, heads * dim), F32)
    for h in range(heads):
        span = 2 * seq
        wing = (span - table) // 2
        low = rel[h : h + 1, : table // 2]
        high = rel[h : h + 1, table // 2 :]
        line = jnp.concatenate(
            [
                high,
                jnp.broadcast_to(rel[h : h + 1, table - 1 :], (1, wing)),
                jnp.broadcast_to(rel[h : h + 1, :1], (1, wing)),
                low,
            ],
            axis=1,
        )
        bias = pltpu.roll(jnp.broadcast_to(line, (half, span)), 0, 1, stride=2, stride_axis=0)[:, :seq]
        raw = nt(jnp.where(head_lanes(half, heads, dim, h), q, 0), k) * 0.125 + bias
        score = jnp.where(allowed, raw, -1e30)
        expo = jnp.exp(score - jnp.max(score, axis=1, keepdims=True))
        p = expo * (1.0 / jnp.sum(expo, axis=1, keepdims=True))
        prob[h] = p
        out = out + nn(p.astype(BF16), jnp.where(head_lanes(seq, heads, dim, h), v, 0))
    low_out = out.astype(BF16)
    ctx[...] = low_out
    hand_out(nn(low_out, wo[...]), keep, send)


def normalise(value):
    centre = value - jnp.mean(value, axis=1, keepdims=True)
    factor = lax.rsqrt(jnp.mean(centre * centre, axis=1, keepdims=True) + 1e-05)
    return centre * factor, factor


def forward(count, b_out, gain, shift, wi, bi, wt, pooled, *refs):
    parts, refs = refs[:count], refs[count:]
    normed_o, factor_o, ylow_o, act_o, slope_o, keep, *send, place = refs
    first = pooled[...] + (gathered(parts, place) + b_out[...])
    normed, factor = normalise(first)
    normed_o[...] = normed
    factor_o[...] = factor
    y_low = (normed * gain[...] + shift[...]).astype(BF16)
    ylow_o[...] = y_low
    inner = nn(y_low, wi[...]) + bi[...]
    cdf = 0.5 + 0.5 * lax.erf(inner * 0.7071067811865476)
    slope_o[...] = cdf + inner * (0.3989422804014327 * jnp.exp(-0.5 * inner * inner))
    act = (inner * cdf).astype(BF16)
    act_o[...] = act
    hand_out(nn(act, wt[...]), keep, send)


def norm_back(grad, normed, factor, gain):
    scaled = grad * gain
    one = jnp.mean(scaled, axis=1, keepdims=True)
    two = jnp.mean(scaled * normed, axis=1, keepdims=True)
    return factor * (scaled - one - normed * two)


def over_rows(value):
    return jnp.sum(value, axis=0, keepdims=True)


def turn(row, count, again, gain_one, shift_one, b_outer, gain, shift, cot, wt, wi, normed_one, slope, *refs):
    parts, refs = refs[:count], refs[count + again :]
    result, g_second_o, g_ffn_o, g_inner_o, small, keep, *send, place, low, done = refs
    y_one = normed_one[...] * gain_one[...] + shift_one[...]
    second = y_one + (gathered(parts, place) + b_outer[...])
    normed, factor = normalise(second)
    low[...] = (normed * gain[...] + shift[...]).astype(BF16)
    leave = pltpu.make_async_copy(low, result.at[row], done)
    leave.start()
    g_out = cot[...].astype(F32)
    g_second = norm_back(g_out, normed, factor, gain[...])
    g_second_o[...] = g_second
    g_ffn = g_second.astype(BF16)
    g_ffn_o[...] = g_ffn
    g_inner = (nt(g_ffn, wt[...]) * slope[...]).astype(BF16)
    g_inner_o[...] = g_inner
    hand_out(nt(g_inner, wi[...]), keep, send)
    small[0:1, :] = over_rows(g_inner.astype(F32))
    small[1:2, :] = over_rows(g_second)
    small[2:3, :] = over_rows(g_out * normed)
    small[3:4, :] = over_rows(g_out)
    leave.wait()


def ffn_weights(kind, lo, hi, act0, act1, g_ffn0, g_ffn1, y0, y1, g_in0, g_in1, *outs):
    def block(ref, lhs0, lhs1, rhs0, rhs1):
        ref[...] = tn(lhs0[:, lo:hi], rhs0[...]) + tn(lhs1[:, lo:hi], rhs1[...])

    outer = (act0, act1, g_ffn0, g_ffn1)
    inner = (y0, y1, g_in0, g_in1)
    if kind == "Z":
        block(outs[0].at[0], *outer)
        block(outs[0].at[1], *inner)
        return
    keep, send = outs

    @pl.when(x_bit() == 0)
    def _():
        block(keep, *outer)
        block(send, *inner)

    @pl.when(x_bit() != 0)
    def _():
        block(keep, *inner)
        block(send, *outer)


def attend_back(heads, count, gain, wo, wq, wk, wv, g_second, normed, factor, q_r, k_r, v_r, prob, *refs):
    parts, refs = refs[:count], refs[count:]
    g_first_o, g_attn_o, gs_o, gq_o, gk_o, gv_o, small, keep, *send, place = refs
    g_y = g_second[...] + gathered(parts, place)
    small[0:1, :] = over_rows(g_y * normed[...])
    small[1:2, :] = over_rows(g_y)
    g_first = norm_back(g_y, normed[...], factor[...], gain[...])
    g_first_o[...] = g_first
    small[2:3, :] = over_rows(g_first)
    g_attn = g_first.astype(BF16)
    g_attn_o[...] = g_attn
    g_ctx = nt(g_attn, wo[...]).astype(BF16)
    q, k, v = q_r[...], k_r[...], v_r[...]
    half, seq = q.shape[0], k.shape[0]
    dim = q.shape[1] // heads
    gq = jnp.zeros(q.shape, F32)
    gk = jnp.zeros(k.shape, F32)
    gv = jnp.zeros(k.shape, F32)
    for h in range(heads):
        own_q = head_lanes(half, heads, dim, h)
        own_k = head_lanes(seq, heads, dim, h)
        g_h = jnp.where(own_q, g_ctx, 0)
        p = prob[h]
        g_p = nt(g_h, v)
        g_s = (p * (g_p - jnp.sum(p * g_p, axis=1, keepdims=True))).astype(BF16)
        gs_o[h] = g_s
        gq = gq + nn(g_s, jnp.where(own_k, k, 0))
        gk = gk + tn(g_s, jnp.where(own_q, q, 0))
        gv = gv + tn(p.astype(BF16), g_h)
    gq = (gq * 0.125).astype(BF16)
    gk = (gk * 0.125).astype(BF16)
    gv = gv.astype(BF16)
    gq_o[...] = gq
    gk_o[...] = gk
    gv_o[...] = gv
    i = lax.broadcasted_iota(jnp.int32, (seq, half), 0)
    j = lax.broadcasted_iota(jnp.int32, (seq, half), 1)
    twice = jnp.where((i >> 1) == j, 0.5, 0.0).astype(BF16)
    gq_twice = nn(twice, gq).astype(BF16)
    hand_out(nn(gk, wk[...]) + nn(gv, wv[...]) + nn(gq_twice, wq[...]), keep, send)


def attn_weights_one(tokens, gq0, gq1, gv0, gv1, pooled0, pooled1, keep, send):
    def queries(ref):
        ref[...] = tn(gq0[...], pooled0[...].astype(BF16)) + tn(gq1[...], pooled1[...].astype(BF16))

    def values(ref):
        ref[...] = tn(gv0[...], tokens[0]) + tn(gv1[...], tokens[1])

    @pl.when(x_bit() == 0)
    def _():
        queries(keep)
        values(send)

    @pl.when(x_bit() != 0)
    def _():
        values(keep)
        queries(send)


def attn_weights_two(heads, table, tokens, gq0, gq1, gk0, gk1, gv0, gv1, ctx0, ctx1, ga0, ga1, gs0, gs1, t0, t1, a0, a1, keep, send):
    seq = tokens.shape[1]
    half, e = gq0.shape
    width = tokens.shape[2]
    i = lax.broadcasted_iota(jnp.int32, (half, half), 0)
    j = lax.broadcasted_iota(jnp.int32, (half, half), 1)
    flip = jnp.where(i + j == half - 1, 1.0, 0.0).astype(BF16)
    lane = lax.broadcasted_iota(jnp.int32, (1, table // 2), 1)
    span = 2 * seq
    pieces = []
    for h in range(heads):
        score = nn(flip, gs0[h]) + nn(flip, gs1[h])
        score = jnp.concatenate([score, jnp.zeros_like(score)], axis=1)
        along = over_rows(pltpu.roll(score, span - 2 * (half - 1), 1, stride=2, stride_axis=0))
        lo = jnp.sum(along[:, seq : span - table // 2], axis=1, keepdims=True)
        hi = jnp.sum(along[:, table // 2 : seq], axis=1, keepdims=True)
        pieces.append(along[:, span - table // 2 :] + jnp.where(lane == 0, lo, 0.0))
        pieces.append(along[:, : table // 2] + jnp.where(lane == table // 2 - 1, hi, 0.0))
    small = [t0[r : r + 1, :] + t1[r : r + 1, :] for r in range(4)]
    small += [a0[r : r + 1, :] + a1[r : r + 1, :] for r in range(3)]
    small.append(jnp.concatenate(pieces, axis=1))
    bq = over_rows(gq0[...].astype(F32)) + over_rows(gq1[...].astype(F32))
    bv = over_rows(gv0[...].astype(F32)) + over_rows(gv1[...].astype(F32))
    last = jnp.concatenate([bq, bv, jnp.zeros((1, width - 2 * e), F32)], axis=1)

    def keys(ref):
        ref[:e, :] = tn(gk0[...], tokens[0]) + tn(gk1[...], tokens[1])
        for r, value in enumerate(small):
            ref[e + r : e + r + 1, :] = value

    def outs(ref):
        ref[:e, :] = tn(ctx0[...], ga0[...]) + tn(ctx1[...], ga1[...])
        ref[e:, :] = jnp.broadcast_to(last, (ref.shape[0] - e, width))

    @pl.when(x_bit() == 0)
    def _():
        keys(keep)
        outs(send)

    @pl.when(x_bit() != 0)
    def _():
        outs(keep)
        keys(send)


def token_end(row, count, again, g_first, *refs):
    parts, refs = refs[:count], refs[count + again :]
    result, place, twice, out, done = refs
    total = gathered(parts, place)
    half = g_first.shape[0]
    for s in range(g_first.shape[1] // 128):
        at = slice(s * 128, (s + 1) * 128)
        value = g_first[:, at] * 0.5
        twice[pl.ds(0, half, stride=2), :] = value
        twice[pl.ds(1, half, stride=2), :] = value
        out[:, at] = (total[:, at] + twice[...]).astype(BF16)
    leave = pltpu.make_async_copy(out, result.at[row], done)
    leave.start()
    leave.wait()


def add(a, b, out):
    out[...] = a[...] + b[...]


def add_split(a, b, keep, send):
    own = centre_half()
    keep[...] = a[own] + b[own]
    send[...] = a[1 - own] + b[1 - own]


def choose(mine, got, out):
    @pl.when(in_centre())
    def _():
        out[...] = mine[...]

    @pl.when(jnp.logical_not(in_centre()))
    def _():
        out[...] = got[...]


def ffn_end(kind, lo, count, *refs):
    parts, (outer, inner, *sems) = refs[:count], refs[-4:]

    def lay(which, low, high):
        @pl.when(which)
        def _():
            copies = [
                pltpu.make_async_copy(part, out.at[lo : lo + part.shape[0]], sem)
                for part, out, sem in zip((low, high), (outer, inner), sems, strict=True)
            ]
            for copy in copies:
                copy.start()
            for copy in copies:
                copy.wait()

    if kind == "X":
        lay(x_bit() == 0, parts[0], parts[1])
        lay(x_bit() != 0, parts[1], parts[0])
        return
    for here, one, two in ((in_centre(), *parts[:2]), (jnp.logical_not(in_centre()), *parts[2:])):
        lay(here & (centre_half() == 0), one, two)
        lay(here & (centre_half() == 1), two, one)


def attn_end_one(final, far, wq, wv):
    def lay(query, value):
        wq[...] = query[...]
        wv[...] = value[...]

    @pl.when(x_bit() == 0)
    def _():
        lay(final, far)

    @pl.when(x_bit() != 0)
    def _():
        lay(far, final)


def attn_end_two(final, far, wk, wo, bq, bv, rel, *small):
    e, width = wk.shape
    heads = rel.shape[0]
    table = width // heads

    def lay(one, two):
        wk[...] = one[:e, :]
        wo[...] = two[:e, :]
        for r, ref in enumerate(small):
            ref[...] = one[e + r, :]
        for h in range(heads):
            rel[h : h + 1, :] = one[e + len(small) : e + len(small) + 1, h * table : (h + 1) * table]
        bq[...] = two[e, :e]
        bv[...] = two[e, e : 2 * e]

    @pl.when(x_bit() == 0)
    def _():
        lay(final, far)

    @pl.when(x_bit() != 0)
    def _():
        lay(far, final)


CHUNKS = [("X", 0, 2), ("X", 2, 3), ("X", 3, 4), ("X", 4, 5), ("Z", 5, 6)]


class TensorSum:
    def __init__(self, run, keep, *send):
        self.run, self.keep, self.got = run, keep, [core_swap(a) for a in send]

    def add(self):
        (self.chip,) = self.run(chip_sum, [shape(self.keep.shape)], [self.keep, *self.got])
        self.far = chip_swap(self.chip)

    def tot(self):
        mine = self.run(total_sum, [shape(a.shape) for a in self.got], [self.chip, self.far])
        self.parts = [*mine, *(core_swap(a) for a in mine)]


def others(a, bit):
    while bit < lax.axis_size("dp"):
        a = a + lax.ppermute(a, "dp", swap_pairs(lax.axis_size("dp"), bit))
        bit *= 2
    return a


class XFirst:
    def __init__(self, run, make):
        self.run, self.make_outs = run, make

    def plus(self, pairs):
        (self.mine,) = self.run(add, [shape(self.mine.shape)], [self.mine, self.got])
        self.got = hop(self.mine, pairs) if on_line_of_four() else None

    def make(self):
        self.mine, send = self.make_outs()
        self.got = x_swap(send)

    def xa(self):
        self.plus(INWARD)

    def ia(self):
        if on_line_of_four():
            self.plus(MIDDLE)

    def ma(self):
        if on_line_of_four():
            self.plus(OUTWARD)

    def ch(self):
        if on_line_of_four():
            (self.mine,) = self.run(choose, [shape(self.mine.shape)], [self.mine, self.got])
        else:
            self.mine = others(self.mine, 2)
        self.parts = [self.mine, x_swap(self.mine)]


class ZFirst:
    def __init__(self, run, make):
        self.run, self.make_outs = run, make

    def make(self):
        (self.whole,) = self.make_outs()
        self.got = hop(self.whole, INWARD) if on_line_of_four() else None

    def ia(self):
        if on_line_of_four():
            half = shape(self.whole.shape[1:])
            self.mine, send = self.run(add_split, [half, half], [self.whole, self.got])
            self.got = hop(send, MIDDLE)

    def ma(self):
        if on_line_of_four():
            (self.mine,) = self.run(add, [shape(self.mine.shape)], [self.mine, self.got])
            self.got = hop(self.mine, CENTRE_X)

    def xa(self):
        if on_line_of_four():
            (mine,) = self.run(add, [shape(self.mine.shape)], [self.mine, self.got])
            other = hop(mine, MIDDLE)
            self.parts = [mine, other, hop(mine, OUTWARD), hop(other, OUTWARD)]
        else:
            total, own = others(self.whole, 1), centre_half() == 0
            pair = [jnp.where(own, total[0], total[1]), jnp.where(own, total[1], total[0])]
            self.parts = pair + pair


def local(
    tokens,
    lengths,
    groups,
    key_mask,
    w_query,
    b_query,
    w_key,
    w_value,
    b_value,
    rel_bias,
    w_out,
    b_out,
    gain_one,
    shift_one,
    w_inner,
    b_inner,
    w_outer,
    b_outer,
    gain_two,
    shift_two,
    cotangent,
):
    rows, seq, width = tokens.shape
    half = seq // 2
    heads, table = rel_bias.shape
    e = w_query.shape[1]
    hidden = w_inner.shape[1]
    w_query, w_key, w_value = w_query.T, w_key.T, w_value.T
    run = Line()
    place = lambda n: pltpu.VMEM((n, width), F32)
    dma = pltpu.SemaphoreType.DMA

    def summands(n, piece=PIECE):
        return [shape((n // 2, width))] + [shape((piece, width))] * (n // 2 // piece)

    class Row:
        output = grad_tokens = None

        def __init__(self, r):
            self.r = r

        def attend(self):
            outs = [
                shape((half, e), BF16),
                shape((half, e), BF16),
                shape((seq, e), BF16),
                shape((seq, e), BF16),
                shape((heads, half, seq)),
                shape((half, width)),
            ]
            late = [lengths, (tokens, self.r), groups, key_mask]
            late += [w_query, b_query, w_key, w_value, b_value, rel_bias, w_out]
            got = run(functools.partial(attend, self.r), outs + summands(half), [], late=late)
            self.ctx, self.q, self.k, self.v, self.prob, self.pooled = got[:6]
            self.att = TensorSum(run, *got[6:])

        def forward(self):
            outs = [
                shape((half, width)),
                shape((half, 1)),
                shape((half, width), BF16),
                shape((half, hidden), BF16),
                shape((half, hidden)),
            ]
            parts = self.att.parts
            got = run(
                functools.partial(forward, len(parts)),
                outs + summands(half),
                [self.pooled, *parts],
                late=[b_out, gain_one, shift_one, w_inner, b_inner, w_outer],
                scratch=[place(half)],
            )
            self.normed, self.factor, self.y_low, self.act, self.slope = got[:5]
            self.ffn = TensorSum(run, *got[5:])

        def turn(self):
            outs = [
                shape((rows, half, width), BF16),
                shape((half, width)),
                shape((half, width), BF16),
                shape((half, hidden), BF16),
                shape((8, width)),
            ]
            parts = self.ffn.parts
            before = [] if Row.output is None else [Row.output]
            got = run(
                functools.partial(turn, self.r, len(parts), len(before)),
                outs + summands(half),
                [self.normed, self.slope, *parts, *before],
                late=[gain_one, shift_one, b_outer, gain_two, shift_two, (cotangent, self.r), w_outer, w_inner],
                scratch=[place(half), pltpu.VMEM((half, width), BF16), dma],
                left=(0,),
                onto=[2 + len(parts)] if before else (),
            )
            Row.output, self.g_second, self.g_ffn, self.g_inner, self.t_small = got[:5]
            self.back = TensorSum(run, *got[5:])

        def aback(self):
            outs = [
                shape((half, width)),
                shape((half, width), BF16),
                shape((heads, half, seq), BF16),
                shape((half, e), BF16),
                shape((seq, e), BF16),
                shape((seq, e), BF16),
                shape((8, width)),
            ]
            parts = self.back.parts
            got = run(
                functools.partial(attend_back, heads, len(parts)),
                outs + summands(seq, seq // 2),
                [self.g_second, self.normed, self.factor, self.q, self.k, self.v, self.prob, *parts],
                late=[gain_one, w_out, w_query, w_key, w_value],
                scratch=[place(half)],
            )
            self.g_first, self.g_attn, self.gs, self.gq, self.gk, self.gv, self.a_small = got[:7]
            self.tok = TensorSum(run, *got[7:])

        def tokend(self):
            parts = self.tok.parts
            before = [] if Row.grad_tokens is None else [Row.grad_tokens]
            (Row.grad_tokens,) = run(
                functools.partial(token_end, self.r, len(parts), len(before)),
                [shape((rows, seq, width), BF16)],
                [self.g_first, *parts, *before],
                scratch=[place(seq), pltpu.VMEM((seq, 128), F32), pltpu.VMEM((seq, width), BF16), dma],
                left=(0,),
                onto=[1 + len(parts)] if before else (),
            )

    r0, r1 = (Row(r) for r in range(rows))

    def ffn_chunk(kind, lo, hi):
        def make():
            outs = [shape((hi - lo, width))] * 2 if kind == "X" else [shape((2, hi - lo, width))]
            ins = [r0.act, r1.act, r0.g_ffn, r1.g_ffn, r0.y_low, r1.y_low, r0.g_inner, r1.g_inner]
            return run(functools.partial(ffn_weights, kind, lo, hi), outs, ins)

        return (XFirst if kind == "X" else ZFirst)(run, make)

    cuts = [(kind, lo * width // 6, hi * width // 6) for kind, lo, hi in CHUNKS]
    chunks = [ffn_chunk(*cut) for cut in cuts]
    x, z = ([chunk for chunk in chunks if isinstance(chunk, kind)] for kind in (XFirst, ZFirst))

    def attn_one():
        ins = [tokens, r0.gq, r1.gq, r0.gv, r1.gv, r0.pooled, r1.pooled]
        return run(attn_weights_one, [shape((e, width))] * 2, ins)

    def attn_two():
        ins = [tokens, r0.gq, r1.gq, r0.gk, r1.gk, r0.gv, r1.gv, r0.ctx, r1.ctx, r0.g_attn, r1.g_attn]
        ins += [r0.gs, r1.gs, r0.t_small, r1.t_small, r0.a_small, r1.a_small]
        return run(functools.partial(attn_weights_two, heads, table), [shape((e + 8, width))] * 2, ins)

    a = [XFirst(run, attn_one), XFirst(run, attn_two)]

    class Ffn:
        grads = ()

    def end(chunk):
        cut = cuts[chunks.index(chunk)]
        outs = [shape((hidden, width)), shape((width, hidden))]
        count = len(chunk.parts)
        Ffn.grads = run(
            functools.partial(ffn_end, *cut[:2], count),
            outs,
            [*chunk.parts, *Ffn.grads],
            scratch=[dma, dma],
            left=(0, 1),
            onto=[count, count + 1] if Ffn.grads else (),
        )

    def aend0():
        return run(attn_end_one, [shape((e, width))] * 2, a[0].parts)

    def aend1():
        outs = [shape((e, width))] * 2 + [shape((e,)), shape((e,)), shape((heads, table))] + [shape((width,))] * 7
        return run(attn_end_two, outs, a[1].parts)

    r0.attend()
    r0.att.add()
    r1.attend()
    r1.att.add()
    r0.att.tot()
    r0.forward()
    r0.ffn.add()
    r1.att.tot()
    r1.forward()
    r1.ffn.add()
    r0.ffn.tot()
    r0.turn()
    r0.back.add()
    r1.ffn.tot()
    r1.turn()
    x[1].make()
    z[0].make()
    x[2].make()
    r1.back.add()
    r0.back.tot()
    x[0].make()
    x[1].xa()
    r0.aback()
    x[2].xa()
    r1.back.tot()
    z[0].ia()
    r1.aback()
    a[0].make()
    x[2].ia()
    z[0].ma()
    r0.tok.add()
    x[0].xa()
    x[1].ia()
    x[2].ma()
    a[1].make()
    x[1].ma()
    a[0].xa()
    x[2].ch()
    x[0].ia()
    x[3].make()
    r0.tok.tot()
    a[1].xa()
    a[0].ia()
    x[3].xa()
    r1.tok.add()
    x[0].ma()
    x[1].ch()
    a[1].ia()
    z[0].xa()
    a[0].ma()
    end(x[2])
    x[0].ch()
    r0.tokend()
    end(x[1])
    a[1].ma()
    a[0].ch()
    x[3].ia()
    end(x[0])
    a[1].ch()
    r1.tok.tot()
    x[3].ma()
    x[3].ch()
    grad_w_query, grad_w_value = aend0()
    grad_w_key, grad_w_out, grad_b_query, grad_b_value, grad_rel_bias, *small = aend1()
    r1.tokend()
    end(z[0])
    end(x[3])
    grad_w_outer, grad_w_inner = Ffn.grads
    grad_b_inner, grad_b_outer, grad_gain_two, grad_shift_two, grad_gain_one, grad_shift_one, grad_b_out = small
    return (
        Row.output,
        Row.grad_tokens,
        grad_w_query.T,
        grad_b_query,
        grad_w_key.T,
        grad_w_value.T,
        grad_b_value,
        grad_rel_bias,
        grad_w_out,
        grad_b_out,
        grad_gain_one,
        grad_shift_one,
        grad_w_inner,
        grad_b_inner,
        grad_w_outer,
        grad_b_outer,
        grad_gain_two,
        grad_shift_two,
    )


def solution(mesh):
    placed = (
        P("dp", None, None),
        P("dp"),
        P("dp", None),
        P("dp", None),
        P(None, "tensor"),
        P("tensor"),
        P(None, "tensor"),
        P(None, "tensor"),
        P("tensor"),
        P("tensor", None),
        P("tensor", None),
        P(),
        P(),
        P(),
        P(None, "tensor"),
        P("tensor"),
        P("tensor", None),
        P(),
        P(),
        P(),
        P("dp", None, None),
    )
    return jax.shard_map(
        local,
        mesh=mesh,
        in_specs=placed,
        out_specs=(
            P("dp", None, None),
            P("dp", None, None),
            P(None, "tensor"),
            P("tensor"),
            P(None, "tensor"),
            P(None, "tensor"),
            P("tensor"),
            P("tensor", None),
            P("tensor", None),
            P(),
            P(),
            P(),
            P(None, "tensor"),
            P("tensor"),
            P("tensor", None),
            P(),
            P(),
            P(),
        ),
        check_vma=False,
    )
```

```python
import functools

import jax
import jax.numpy as jnp
from jax import lax
from jax.experimental import pallas as pl
from jax.experimental.pallas import tpu as pltpu
from jax.sharding import PartitionSpec as P

F32 = jnp.float32
BF16 = jnp.bfloat16
VMEM_BYTES = 12 << 20
PIECE = 32

INWARD = [(0, 2), (1, 3), (6, 4), (7, 5)]
MIDDLE = [(2, 4), (3, 5), (4, 2), (5, 3)]
OUTWARD = [(2, 0), (3, 1), (4, 6), (5, 7)]
CENTRE_X = [(2, 3), (3, 2), (4, 5), (5, 4)]
OUTER_X = [(0, 1), (1, 0), (6, 7), (7, 6)]


def swap_pairs(n, bit):
    return [(i, i ^ bit) for i in range(n)]


def core_swap(a):
    return lax.ppermute(a, "tensor", swap_pairs(lax.axis_size("tensor"), 1))


def chip_swap(a):
    return lax.ppermute(a, "tensor", swap_pairs(lax.axis_size("tensor"), 2))


def x_swap(a):
    return lax.ppermute(a, "dp", swap_pairs(lax.axis_size("dp"), 1))


def hop(a, pairs):
    return lax.ppermute(a, "dp", pairs)


def on_line_of_four():
    return lax.axis_size("dp") == 8


def core_bit():
    return lax.axis_index("tensor") & 1


def x_bit():
    return lax.axis_index("dp") & 1


def centre_half():
    return ((lax.axis_index("dp") >> 1) >= 2).astype(jnp.int32)


def in_centre():
    z = lax.axis_index("dp") >> 1
    return (z == 1) | (z == 2)


def nn(a, b):
    return jnp.dot(a, b, preferred_element_type=F32)


def nt(a, b):
    return lax.dot_general(a, b, (((1,), (1,)), ((), ())), preferred_element_type=F32)


def tn(a, b):
    return lax.dot_general(a, b, (((0,), (0,)), ((), ())), preferred_element_type=F32)


def shape(dims, dtype=F32):
    return jax.ShapeDtypeStruct(dims, dtype)


ANY = pl.BlockSpec(memory_space=pl.ANY)
VMEM = pl.BlockSpec(memory_space=pltpu.VMEM)


class View:
    def __init__(self, ref, pick):
        self.ref = ref if pick is None else ref.at[pick]
        self.shape = self.ref.shape

    def __getitem__(self, at):
        value = self.ref[at]
        return value.reshape(1, -1) if len(self.shape) == 1 and at is Ellipsis else value


def begin(token):
    token[...] = jnp.zeros_like(token)


class Line:
    def __init__(self):
        self.token = pl.pallas_call(
            begin,
            out_specs=VMEM,
            out_shape=shape((8, 128)),
            cost_estimate=pl.CostEstimate(flops=1 << 31, bytes_accessed=1 << 20, transcendentals=0),
        )()

    def __call__(self, body, outs, ins, late=(), scratch=(), left=(), onto=()):
        late = [item if isinstance(item, tuple) else (item, None) for item in late]
        far, near, given = len(late), len(ins), len(outs)

        def kernel(*refs):
            views = [View(ref, pick) for ref, (_, pick) in zip(refs, late, strict=False)]
            rest = refs[far + near + 1 :]
            body(*views, *refs[far : far + near], *rest[:given], *rest[given + 1 :])

        result = pl.pallas_call(
            kernel,
            name=getattr(body, "func", body).__name__,
            in_specs=[VMEM] * far
            + [ANY if i in onto else VMEM for i in range(near)]
            + [ANY],
            out_specs=[ANY if i in left else VMEM for i in range(given)] + [ANY],
            out_shape=[*outs, shape(self.token.shape)],
            scratch_shapes=list(scratch),
            input_output_aliases={far + i: o for i, o in zip(onto, left, strict=False)},
            compiler_params=pltpu.CompilerParams(vmem_limit_bytes=VMEM_BYTES),
            cost_estimate=pl.CostEstimate(flops=1024, bytes_accessed=1024, transcendentals=0),
        )(*(a for a, _ in late), *ins, self.token)
        self.token = result[-1]
        return result[:-1]


def hand_out(value, keep, send):
    size = keep.shape[0]
    for core in range(2):

        @pl.when(core_bit() == core)
        def _(core=core):
            keep[...] = value[core * size : (core + 1) * size]
            at = (1 - core) * size
            for ref in send:
                ref[...] = value[at : at + ref.shape[0]]
                at += ref.shape[0]


def chip_sum(keep, *refs):
    *got, out = refs
    size = got[0].shape[0]
    for i, ref in enumerate(got):
        at = slice(i * size, (i + 1) * size)
        out[at, :] = keep[at, :] + ref[...]


def total_sum(chip, far, *outs):
    size = outs[0].shape[0]
    for i, ref in enumerate(outs):
        at = slice(i * size, (i + 1) * size)
        ref[...] = chip[at, :] + far[at, :]


def gathered(parts, place):
    size, piece = place.shape[0] // 2, parts[0].shape[0]
    core = core_bit()
    for side, own in ((core, parts[: len(parts) // 2]), (1 - core, parts[len(parts) // 2 :])):
        for i, ref in enumerate(own):
            place[pl.ds(pl.multiple_of(side * size + i * piece, piece), piece), :] = ref[...]
    return place[...]


def head_lanes(size, heads, dim, h):
    lane = lax.broadcasted_iota(jnp.int32, (size, heads * dim), 1)
    return (lane >= h * dim) & (lane < (h + 1) * dim)


def attend(row, lens, tokens, groups, key_mask, wq, bq, wk, wv, bv, rel, wo, ctx, qo, ko, vo, prob, pooled_out, keep, *send):
    heads, table = rel.shape
    seq = tokens.shape[0]
    half = seq // 2
    dim = wq.shape[0] // heads
    tok = tokens[...]
    i = lax.broadcasted_iota(jnp.int32, (half, seq), 0)
    j = lax.broadcasted_iota(jnp.int32, (half, seq), 1)
    pick = jnp.where((j >> 1) == i, 0.5, 0.0).astype(BF16)
    pooled = nn(pick, tok)
    pooled_out[...] = pooled
    q = (nt(pooled.astype(BF16), wq[...]) + bq[...]).astype(BF16)
    k = nt(tok, wk[...]).astype(BF16)
    v = (nt(tok, wv[...]) + bv[...]).astype(BF16)
    qo[...] = q
    ko[...] = k
    vo[...] = v
    self_key = j == 2 * i
    group = groups[row : row + 1, :].astype(F32)
    place = lax.broadcasted_iota(jnp.int32, (1, seq), 1)
    live = (place < lens[...][:, row : row + 1]) & (key_mask[row : row + 1, :] == 1)
    own = jnp.sum(jnp.where(self_key, group, 0.0), axis=1, keepdims=True)
    allowed = self_key | (own == jnp.where(live, group, -1.0))
    out = jnp.zeros((half, heads * dim), F32)
    for h in range(heads):
        span = 2 * seq
        wing = (span - table) // 2
        low = rel[h : h + 1, : table // 2]
        high = rel[h : h + 1, table // 2 :]
        line = jnp.concatenate(
            [
                high,
                jnp.broadcast_to(rel[h : h + 1, table - 1 :], (1, wing)),
                jnp.broadcast_to(rel[h : h + 1, :1], (1, wing)),
                low,
            ],
            axis=1,
        )
        bias = pltpu.roll(jnp.broadcast_to(line, (half, span)), 0, 1, stride=2, stride_axis=0)[:, :seq]
        raw = nt(jnp.where(head_lanes(half, heads, dim, h), q, 0), k) * 0.125 + bias
        score = jnp.where(allowed, raw, -1e30)
        expo = jnp.exp(score - jnp.max(score, axis=1, keepdims=True))
        p = expo * (1.0 / jnp.sum(expo, axis=1, keepdims=True))
        prob[h] = p
        out = out + nn(p.astype(BF16), jnp.where(head_lanes(seq, heads, dim, h), v, 0))
    low_out = out.astype(BF16)
    ctx[...] = low_out
    hand_out(nn(low_out, wo[...]), keep, send)


def normalise(value):
    centre = value - jnp.mean(value, axis=1, keepdims=True)
    factor = lax.rsqrt(jnp.mean(centre * centre, axis=1, keepdims=True) + 1e-05)
    return centre * factor, factor


def forward(count, b_out, gain, shift, wi, bi, wt, pooled, *refs):
    parts, refs = refs[:count], refs[count:]
    normed_o, factor_o, ylow_o, act_o, slope_o, keep, *send, place = refs
    first = pooled[...] + (gathered(parts, place) + b_out[...])
    normed, factor = normalise(first)
    normed_o[...] = normed
    factor_o[...] = factor
    y_low = (normed * gain[...] + shift[...]).astype(BF16)
    ylow_o[...] = y_low
    inner = nn(y_low, wi[...]) + bi[...]
    cdf = 0.5 + 0.5 * lax.erf(inner * 0.7071067811865476)
    slope_o[...] = cdf + inner * (0.3989422804014327 * jnp.exp(-0.5 * inner * inner))
    act = (inner * cdf).astype(BF16)
    act_o[...] = act
    hand_out(nn(act, wt[...]), keep, send)


def norm_back(grad, normed, factor, gain):
    scaled = grad * gain
    one = jnp.mean(scaled, axis=1, keepdims=True)
    two = jnp.mean(scaled * normed, axis=1, keepdims=True)
    return factor * (scaled - one - normed * two)


def over_rows(value):
    return jnp.sum(value, axis=0, keepdims=True)


def turn(row, count, again, gain_one, shift_one, b_outer, gain, shift, cot, wt, wi, normed_one, slope, *refs):
    parts, refs = refs[:count], refs[count + again :]
    result, g_second_o, g_ffn_o, g_inner_o, small, keep, *send, place, low, done = refs
    y_one = normed_one[...] * gain_one[...] + shift_one[...]
    second = y_one + (gathered(parts, place) + b_outer[...])
    normed, factor = normalise(second)
    low[...] = (normed * gain[...] + shift[...]).astype(BF16)
    leave = pltpu.make_async_copy(low, result.at[row], done)
    leave.start()
    g_out = cot[...].astype(F32)
    g_second = norm_back(g_out, normed, factor, gain[...])
    g_second_o[...] = g_second
    g_ffn = g_second.astype(BF16)
    g_ffn_o[...] = g_ffn
    g_inner = (nt(g_ffn, wt[...]) * slope[...]).astype(BF16)
    g_inner_o[...] = g_inner
    hand_out(nt(g_inner, wi[...]), keep, send)
    small[0:1, :] = over_rows(g_inner.astype(F32))
    small[1:2, :] = over_rows(g_second)
    small[2:3, :] = over_rows(g_out * normed)
    small[3:4, :] = over_rows(g_out)
    leave.wait()


def ffn_weights(kind, lo, hi, act0, act1, g_ffn0, g_ffn1, y0, y1, g_in0, g_in1, *outs):
    def block(ref, lhs0, lhs1, rhs0, rhs1):
        ref[...] = tn(lhs0[:, lo:hi], rhs0[...]) + tn(lhs1[:, lo:hi], rhs1[...])

    outer = (act0, act1, g_ffn0, g_ffn1)
    inner = (y0, y1, g_in0, g_in1)
    if kind == "Z":
        block(outs[0].at[0], *outer)
        block(outs[0].at[1], *inner)
        return
    keep, send = outs

    @pl.when(x_bit() == 0)
    def _():
        block(keep, *outer)
        block(send, *inner)

    @pl.when(x_bit() != 0)
    def _():
        block(keep, *inner)
        block(send, *outer)


def attend_back(heads, count, gain, wo, wq, wk, wv, g_second, normed, factor, q_r, k_r, v_r, prob, *refs):
    parts, refs = refs[:count], refs[count:]
    g_first_o, g_attn_o, gs_o, gq_o, gk_o, gv_o, small, keep, *send, place = refs
    g_y = g_second[...] + gathered(parts, place)
    small[0:1, :] = over_rows(g_y * normed[...])
    small[1:2, :] = over_rows(g_y)
    g_first = norm_back(g_y, normed[...], factor[...], gain[...])
    g_first_o[...] = g_first
    small[2:3, :] = over_rows(g_first)
    g_attn = g_first.astype(BF16)
    g_attn_o[...] = g_attn
    g_ctx = nt(g_attn, wo[...]).astype(BF16)
    q, k, v = q_r[...], k_r[...], v_r[...]
    half, seq = q.shape[0], k.shape[0]
    dim = q.shape[1] // heads
    gq = jnp.zeros(q.shape, F32)
    gk = jnp.zeros(k.shape, F32)
    gv = jnp.zeros(k.shape, F32)
    for h in range(heads):
        own_q = head_lanes(half, heads, dim, h)
        own_k = head_lanes(seq, heads, dim, h)
        g_h = jnp.where(own_q, g_ctx, 0)
        p = prob[h]
        g_p = nt(g_h, v)
        g_s = (p * (g_p - jnp.sum(p * g_p, axis=1, keepdims=True))).astype(BF16)
        gs_o[h] = g_s
        gq = gq + nn(g_s, jnp.where(own_k, k, 0))
        gk = gk + tn(g_s, jnp.where(own_q, q, 0))
        gv = gv + tn(p.astype(BF16), g_h)
    gq = (gq * 0.125).astype(BF16)
    gk = (gk * 0.125).astype(BF16)
    gv = gv.astype(BF16)
    gq_o[...] = gq
    gk_o[...] = gk
    gv_o[...] = gv
    i = lax.broadcasted_iota(jnp.int32, (seq, half), 0)
    j = lax.broadcasted_iota(jnp.int32, (seq, half), 1)
    twice = jnp.where((i >> 1) == j, 0.5, 0.0).astype(BF16)
    gq_twice = nn(twice, gq).astype(BF16)
    hand_out(nn(gk, wk[...]) + nn(gv, wv[...]) + nn(gq_twice, wq[...]), keep, send)


def attn_weights_one(tokens, gq0, gq1, gv0, gv1, pooled0, pooled1, keep, send):
    def queries(ref):
        ref[...] = tn(gq0[...], pooled0[...].astype(BF16)) + tn(gq1[...], pooled1[...].astype(BF16))

    def values(ref):
        ref[...] = tn(gv0[...], tokens[0]) + tn(gv1[...], tokens[1])

    @pl.when(x_bit() == 0)
    def _():
        queries(keep)
        values(send)

    @pl.when(x_bit() != 0)
    def _():
        values(keep)
        queries(send)


def attn_weights_two(heads, table, tokens, gq0, gq1, gk0, gk1, gv0, gv1, ctx0, ctx1, ga0, ga1, gs0, gs1, t0, t1, a0, a1, keep, send):
    seq = tokens.shape[1]
    half, e = gq0.shape
    width = tokens.shape[2]
    i = lax.broadcasted_iota(jnp.int32, (half, half), 0)
    j = lax.broadcasted_iota(jnp.int32, (half, half), 1)
    flip = jnp.where(i + j == half - 1, 1.0, 0.0).astype(BF16)
    lane = lax.broadcasted_iota(jnp.int32, (1, table // 2), 1)
    span = 2 * seq
    pieces = []
    for h in range(heads):
        score = nn(flip, gs0[h]) + nn(flip, gs1[h])
        score = jnp.concatenate([score, jnp.zeros_like(score)], axis=1)
        along = over_rows(pltpu.roll(score, span - 2 * (half - 1), 1, stride=2, stride_axis=0))
        lo = jnp.sum(along[:, seq : span - table // 2], axis=1, keepdims=True)
        hi = jnp.sum(along[:, table // 2 : seq], axis=1, keepdims=True)
        pieces.append(along[:, span - table // 2 :] + jnp.where(lane == 0, lo, 0.0))
        pieces.append(along[:, : table // 2] + jnp.where(lane == table // 2 - 1, hi, 0.0))
    small = [t0[r : r + 1, :] + t1[r : r + 1, :] for r in range(4)]
    small += [a0[r : r + 1, :] + a1[r : r + 1, :] for r in range(3)]
    small.append(jnp.concatenate(pieces, axis=1))
    bq = over_rows(gq0[...].astype(F32)) + over_rows(gq1[...].astype(F32))
    bv = over_rows(gv0[...].astype(F32)) + over_rows(gv1[...].astype(F32))
    last = jnp.concatenate([bq, bv, jnp.zeros((1, width - 2 * e), F32)], axis=1)

    def keys(ref):
        ref[:e, :] = tn(gk0[...], tokens[0]) + tn(gk1[...], tokens[1])
        for r, value in enumerate(small):
            ref[e + r : e + r + 1, :] = value

    def outs(ref):
        ref[:e, :] = tn(ctx0[...], ga0[...]) + tn(ctx1[...], ga1[...])
        ref[e:, :] = jnp.broadcast_to(last, (ref.shape[0] - e, width))

    @pl.when(x_bit() == 0)
    def _():
        keys(keep)
        outs(send)

    @pl.when(x_bit() != 0)
    def _():
        outs(keep)
        keys(send)


def token_end(row, count, again, g_first, *refs):
    parts, refs = refs[:count], refs[count + again :]
    result, place, twice, out, done = refs
    total = gathered(parts, place)
    half = g_first.shape[0]
    for s in range(g_first.shape[1] // 128):
        at = slice(s * 128, (s + 1) * 128)
        value = g_first[:, at] * 0.5
        twice[pl.ds(0, half, stride=2), :] = value
        twice[pl.ds(1, half, stride=2), :] = value
        out[:, at] = (total[:, at] + twice[...]).astype(BF16)
    leave = pltpu.make_async_copy(out, result.at[row], done)
    leave.start()
    leave.wait()


def add(a, b, out):
    out[...] = a[...] + b[...]


def add_split(a, b, keep, send):
    own = centre_half()
    keep[...] = a[own] + b[own]
    send[...] = a[1 - own] + b[1 - own]


def choose(mine, got, out):
    @pl.when(in_centre())
    def _():
        out[...] = mine[...]

    @pl.when(jnp.logical_not(in_centre()))
    def _():
        out[...] = got[...]


def ffn_end(kind, lo, count, *refs):
    parts, (outer, inner, *sems) = refs[:count], refs[-4:]

    def lay(which, low, high):
        @pl.when(which)
        def _():
            copies = [
                pltpu.make_async_copy(part, out.at[lo : lo + part.shape[0]], sem)
                for part, out, sem in zip((low, high), (outer, inner), sems, strict=True)
            ]
            for copy in copies:
                copy.start()
            for copy in copies:
                copy.wait()

    if kind == "X":
        lay(x_bit() == 0, parts[0], parts[1])
        lay(x_bit() != 0, parts[1], parts[0])
        return
    if kind == "V":
        for here, far in ((in_centre(), parts[2]), (jnp.logical_not(in_centre()), parts[1])):
            lay(here & (x_bit() == 0), parts[0], far)
            lay(here & (x_bit() != 0), far, parts[0])
        return
    for here, one, two in ((in_centre(), *parts[:2]), (jnp.logical_not(in_centre()), *parts[2:])):
        lay(here & (centre_half() == 0), one, two)
        lay(here & (centre_half() == 1), two, one)


def attn_end_one(final, far, wq, wv):
    def lay(query, value):
        wq[...] = query[...]
        wv[...] = value[...]

    @pl.when(x_bit() == 0)
    def _():
        lay(final, far)

    @pl.when(x_bit() != 0)
    def _():
        lay(far, final)


def attn_end_two(final, far, wk, wo, bq, bv, rel, *small):
    e, width = wk.shape
    heads = rel.shape[0]
    table = width // heads

    def lay(one, two):
        wk[...] = one[:e, :]
        wo[...] = two[:e, :]
        for r, ref in enumerate(small):
            ref[...] = one[e + r, :]
        for h in range(heads):
            rel[h : h + 1, :] = one[e + len(small) : e + len(small) + 1, h * table : (h + 1) * table]
        bq[...] = two[e, :e]
        bv[...] = two[e, e : 2 * e]

    @pl.when(x_bit() == 0)
    def _():
        lay(final, far)

    @pl.when(x_bit() != 0)
    def _():
        lay(far, final)


CHUNKS = [("X", 0, 2), ("V", 2, 4), ("X", 4, 5), ("Z", 5, 6)]


class TensorSum:
    def __init__(self, run, keep, *send):
        self.run, self.keep, self.got = run, keep, [core_swap(a) for a in send]

    def add(self):
        (self.chip,) = self.run(chip_sum, [shape(self.keep.shape)], [self.keep, *self.got])
        self.far = chip_swap(self.chip)

    def tot(self):
        mine = self.run(total_sum, [shape(a.shape) for a in self.got], [self.chip, self.far])
        self.parts = [*mine, *(core_swap(a) for a in mine)]


def others(a, bit):
    while bit < lax.axis_size("dp"):
        a = a + lax.ppermute(a, "dp", swap_pairs(lax.axis_size("dp"), bit))
        bit *= 2
    return a


class XFirst:
    def __init__(self, run, make):
        self.run, self.make_outs = run, make

    def plus(self, pairs):
        (self.mine,) = self.run(add, [shape(self.mine.shape)], [self.mine, self.got])
        self.got = hop(self.mine, pairs) if on_line_of_four() else None

    def make(self):
        self.mine, send = self.make_outs()
        self.got = x_swap(send)

    def xa(self):
        self.plus(INWARD)

    def ia(self):
        if on_line_of_four():
            self.plus(MIDDLE)

    def ma(self):
        if on_line_of_four():
            self.plus(OUTWARD)

    def ch(self):
        if on_line_of_four():
            (self.mine,) = self.run(choose, [shape(self.mine.shape)], [self.mine, self.got])
        else:
            self.mine = others(self.mine, 2)
        self.parts = [self.mine, x_swap(self.mine)]


class XOuter(XFirst):
    def ch(self):
        if not on_line_of_four():
            super().ch()
            self.parts.append(self.parts[1])
            return
        (self.mine,) = self.run(choose, [shape(self.mine.shape)], [self.mine, self.got])
        other = hop(self.mine, OUTER_X)
        self.parts = [self.mine, other, hop(other, INWARD)]


class ZFirst:
    def __init__(self, run, make):
        self.run, self.make_outs = run, make

    def make(self):
        (self.whole,) = self.make_outs()
        self.got = hop(self.whole, INWARD) if on_line_of_four() else None

    def ia(self):
        if on_line_of_four():
            half = shape(self.whole.shape[1:])
            self.mine, send = self.run(add_split, [half, half], [self.whole, self.got])
            self.got = hop(send, MIDDLE)

    def ma(self):
        if on_line_of_four():
            (self.mine,) = self.run(add, [shape(self.mine.shape)], [self.mine, self.got])
            self.got = hop(self.mine, CENTRE_X)

    def xa(self):
        if on_line_of_four():
            (mine,) = self.run(add, [shape(self.mine.shape)], [self.mine, self.got])
            other = hop(mine, MIDDLE)
            self.parts = [mine, other, hop(mine, OUTWARD), hop(other, OUTWARD)]
        else:
            total, own = others(self.whole, 1), centre_half() == 0
            pair = [jnp.where(own, total[0], total[1]), jnp.where(own, total[1], total[0])]
            self.parts = pair + pair


def local(
    tokens,
    lengths,
    groups,
    key_mask,
    w_query,
    b_query,
    w_key,
    w_value,
    b_value,
    rel_bias,
    w_out,
    b_out,
    gain_one,
    shift_one,
    w_inner,
    b_inner,
    w_outer,
    b_outer,
    gain_two,
    shift_two,
    cotangent,
):
    rows, seq, width = tokens.shape
    half = seq // 2
    heads, table = rel_bias.shape
    e = w_query.shape[1]
    hidden = w_inner.shape[1]
    w_query, w_key, w_value = w_query.T, w_key.T, w_value.T
    run = Line()
    place = lambda n: pltpu.VMEM((n, width), F32)
    dma = pltpu.SemaphoreType.DMA

    def summands(n, piece=PIECE):
        return [shape((n // 2, width))] + [shape((piece, width))] * (n // 2 // piece)

    class Row:
        output = grad_tokens = None

        def __init__(self, r):
            self.r = r

        def attend(self):
            outs = [
                shape((half, e), BF16),
                shape((half, e), BF16),
                shape((seq, e), BF16),
                shape((seq, e), BF16),
                shape((heads, half, seq)),
                shape((half, width)),
            ]
            late = [lengths, (tokens, self.r), groups, key_mask]
            late += [w_query, b_query, w_key, w_value, b_value, rel_bias, w_out]
            got = run(functools.partial(attend, self.r), outs + summands(half), [], late=late)
            self.ctx, self.q, self.k, self.v, self.prob, self.pooled = got[:6]
            self.att = TensorSum(run, *got[6:])

        def forward(self):
            outs = [
                shape((half, width)),
                shape((half, 1)),
                shape((half, width), BF16),
                shape((half, hidden), BF16),
                shape((half, hidden)),
            ]
            parts = self.att.parts
            got = run(
                functools.partial(forward, len(parts)),
                outs + summands(half),
                [self.pooled, *parts],
                late=[b_out, gain_one, shift_one, w_inner, b_inner, w_outer],
                scratch=[place(half)],
            )
            self.normed, self.factor, self.y_low, self.act, self.slope = got[:5]
            self.ffn = TensorSum(run, *got[5:])

        def turn(self):
            outs = [
                shape((rows, half, width), BF16),
                shape((half, width)),
                shape((half, width), BF16),
                shape((half, hidden), BF16),
                shape((8, width)),
            ]
            parts = self.ffn.parts
            before = [] if Row.output is None else [Row.output]
            got = run(
                functools.partial(turn, self.r, len(parts), len(before)),
                outs + summands(half),
                [self.normed, self.slope, *parts, *before],
                late=[gain_one, shift_one, b_outer, gain_two, shift_two, (cotangent, self.r), w_outer, w_inner],
                scratch=[place(half), pltpu.VMEM((half, width), BF16), dma],
                left=(0,),
                onto=[2 + len(parts)] if before else (),
            )
            Row.output, self.g_second, self.g_ffn, self.g_inner, self.t_small = got[:5]
            self.back = TensorSum(run, *got[5:])

        def aback(self):
            outs = [
                shape((half, width)),
                shape((half, width), BF16),
                shape((heads, half, seq), BF16),
                shape((half, e), BF16),
                shape((seq, e), BF16),
                shape((seq, e), BF16),
                shape((8, width)),
            ]
            parts = self.back.parts
            got = run(
                functools.partial(attend_back, heads, len(parts)),
                outs + summands(seq, seq // 2),
                [self.g_second, self.normed, self.factor, self.q, self.k, self.v, self.prob, *parts],
                late=[gain_one, w_out, w_query, w_key, w_value],
                scratch=[place(half)],
            )
            self.g_first, self.g_attn, self.gs, self.gq, self.gk, self.gv, self.a_small = got[:7]
            self.tok = TensorSum(run, *got[7:])

        def tokend(self):
            parts = self.tok.parts
            before = [] if Row.grad_tokens is None else [Row.grad_tokens]
            (Row.grad_tokens,) = run(
                functools.partial(token_end, self.r, len(parts), len(before)),
                [shape((rows, seq, width), BF16)],
                [self.g_first, *parts, *before],
                scratch=[place(seq), pltpu.VMEM((seq, 128), F32), pltpu.VMEM((seq, width), BF16), dma],
                left=(0,),
                onto=[1 + len(parts)] if before else (),
            )

    r0, r1 = (Row(r) for r in range(rows))

    def ffn_chunk(kind, lo, hi):
        def make():
            outs = [shape((2, hi - lo, width))] if kind == "Z" else [shape((hi - lo, width))] * 2
            ins = [r0.act, r1.act, r0.g_ffn, r1.g_ffn, r0.y_low, r1.y_low, r0.g_inner, r1.g_inner]
            return run(functools.partial(ffn_weights, kind, lo, hi), outs, ins)

        return {"X": XFirst, "V": XOuter, "Z": ZFirst}[kind](run, make)

    cuts = [(kind, lo * width // 6, hi * width // 6) for kind, lo, hi in CHUNKS]
    chunks = [ffn_chunk(*cut) for cut in cuts]
    x, v, z = ([chunk for chunk in chunks if type(chunk) is kind] for kind in (XFirst, XOuter, ZFirst))

    def attn_one():
        ins = [tokens, r0.gq, r1.gq, r0.gv, r1.gv, r0.pooled, r1.pooled]
        return run(attn_weights_one, [shape((e, width))] * 2, ins)

    def attn_two():
        ins = [tokens, r0.gq, r1.gq, r0.gk, r1.gk, r0.gv, r1.gv, r0.ctx, r1.ctx, r0.g_attn, r1.g_attn]
        ins += [r0.gs, r1.gs, r0.t_small, r1.t_small, r0.a_small, r1.a_small]
        return run(functools.partial(attn_weights_two, heads, table), [shape((e + 8, width))] * 2, ins)

    a = [XFirst(run, attn_one), XFirst(run, attn_two)]

    class Ffn:
        grads = ()

    def end(chunk):
        cut = cuts[chunks.index(chunk)]
        outs = [shape((hidden, width)), shape((width, hidden))]
        count = len(chunk.parts)
        Ffn.grads = run(
            functools.partial(ffn_end, *cut[:2], count),
            outs,
            [*chunk.parts, *Ffn.grads],
            scratch=[dma, dma],
            left=(0, 1),
            onto=[count, count + 1] if Ffn.grads else (),
        )

    def aend0():
        return run(attn_end_one, [shape((e, width))] * 2, a[0].parts)

    def aend1():
        outs = [shape((e, width))] * 2 + [shape((e,)), shape((e,)), shape((heads, table))] + [shape((width,))] * 7
        return run(attn_end_two, outs, a[1].parts)

    r0.attend()
    r0.att.add()
    r1.attend()
    r1.att.add()
    r0.att.tot()
    r0.forward()
    r0.ffn.add()
    r1.att.tot()
    r1.forward()
    r1.ffn.add()
    r0.ffn.tot()
    r0.turn()
    r0.back.add()
    r1.ffn.tot()
    r1.turn()
    v[0].make()
    z[0].make()
    x[0].make()
    r0.back.tot()
    r0.aback()
    r1.back.add()
    v[0].xa()
    r1.back.tot()
    z[0].ia()
    r1.aback()
    r0.tok.add()
    a[0].make()
    x[0].xa()
    z[0].ma()
    v[0].ia()
    a[1].make()
    x[1].make()
    r0.tok.tot()
    a[0].xa()
    r1.tok.add()
    x[0].ia()
    v[0].ma()
    a[1].xa()
    a[0].ia()
    r1.tok.tot()
    x[0].ma()
    x[1].xa()
    v[0].ch()
    a[1].ia()
    a[0].ma()
    z[0].xa()
    x[1].ia()
    x[0].ch()
    a[1].ma()
    a[0].ch()
    end(x[0])
    r0.tokend()
    x[1].ma()
    end(v[0])
    a[1].ch()
    x[1].ch()
    grad_w_query, grad_w_value = aend0()
    grad_w_key, grad_w_out, grad_b_query, grad_b_value, grad_rel_bias, *small = aend1()
    end(z[0])
    r1.tokend()
    end(x[1])
    grad_w_outer, grad_w_inner = Ffn.grads
    grad_b_inner, grad_b_outer, grad_gain_two, grad_shift_two, grad_gain_one, grad_shift_one, grad_b_out = small
    return (
        Row.output,
        Row.grad_tokens,
        grad_w_query.T,
        grad_b_query,
        grad_w_key.T,
        grad_w_value.T,
        grad_b_value,
        grad_rel_bias,
        grad_w_out,
        grad_b_out,
        grad_gain_one,
        grad_shift_one,
        grad_w_inner,
        grad_b_inner,
        grad_w_outer,
        grad_b_outer,
        grad_gain_two,
        grad_shift_two,
    )


def solution(mesh):
    placed = (
        P("dp", None, None),
        P("dp"),
        P("dp", None),
        P("dp", None),
        P(None, "tensor"),
        P("tensor"),
        P(None, "tensor"),
        P(None, "tensor"),
        P("tensor"),
        P("tensor", None),
        P("tensor", None),
        P(),
        P(),
        P(),
        P(None, "tensor"),
        P("tensor"),
        P("tensor", None),
        P(),
        P(),
        P(),
        P("dp", None, None),
    )
    return jax.shard_map(
        local,
        mesh=mesh,
        in_specs=placed,
        out_specs=(
            P("dp", None, None),
            P("dp", None, None),
            P(None, "tensor"),
            P("tensor"),
            P(None, "tensor"),
            P(None, "tensor"),
            P("tensor"),
            P("tensor", None),
            P("tensor", None),
            P(),
            P(),
            P(),
            P(None, "tensor"),
            P("tensor"),
            P("tensor", None),
            P(),
            P(),
            P(),
        ),
        check_vma=False,
    )
```

```python
import functools

import jax
import jax.numpy as jnp
from jax import lax
from jax.experimental import pallas as pl
from jax.experimental.pallas import tpu as pltpu
from jax.sharding import PartitionSpec as P

F32 = jnp.float32
BF16 = jnp.bfloat16
VMEM_BYTES = 12 << 20
PIECE = 32

INWARD = [(0, 2), (1, 3), (6, 4), (7, 5)]
MIDDLE = [(2, 4), (3, 5), (4, 2), (5, 3)]
OUTWARD = [(2, 0), (3, 1), (4, 6), (5, 7)]
CENTRE_X = [(2, 3), (3, 2), (4, 5), (5, 4)]
OUTER_X = [(0, 1), (1, 0), (6, 7), (7, 6)]


def swap_pairs(n, bit):
    return [(i, i ^ bit) for i in range(n)]


def core_swap(a):
    return lax.ppermute(a, "tensor", swap_pairs(lax.axis_size("tensor"), 1))


def chip_swap(a):
    return lax.ppermute(a, "tensor", swap_pairs(lax.axis_size("tensor"), 2))


def x_swap(a):
    return lax.ppermute(a, "dp", swap_pairs(lax.axis_size("dp"), 1))


def hop(a, pairs):
    return lax.ppermute(a, "dp", pairs)


def on_line_of_four():
    return lax.axis_size("dp") == 8


def core_bit():
    return lax.axis_index("tensor") & 1


def x_bit():
    return lax.axis_index("dp") & 1


def centre_half():
    return ((lax.axis_index("dp") >> 1) >= 2).astype(jnp.int32)


def in_centre():
    z = lax.axis_index("dp") >> 1
    return (z == 1) | (z == 2)


def nn(a, b):
    return jnp.dot(a, b, preferred_element_type=F32)


def nt(a, b):
    return lax.dot_general(a, b, (((1,), (1,)), ((), ())), preferred_element_type=F32)


def tn(a, b):
    return lax.dot_general(a, b, (((0,), (0,)), ((), ())), preferred_element_type=F32)


def shape(dims, dtype=F32):
    return jax.ShapeDtypeStruct(dims, dtype)


ANY = pl.BlockSpec(memory_space=pl.ANY)
VMEM = pl.BlockSpec(memory_space=pltpu.VMEM)


class View:
    def __init__(self, ref, pick):
        self.ref = ref if pick is None else ref.at[pick]
        self.shape = self.ref.shape

    def __getitem__(self, at):
        value = self.ref[at]
        return value.reshape(1, -1) if len(self.shape) == 1 and at is Ellipsis else value


def begin(token):
    token[...] = jnp.zeros_like(token)


class Line:
    def __init__(self):
        self.token = pl.pallas_call(
            begin,
            out_specs=VMEM,
            out_shape=shape((8, 128)),
            cost_estimate=pl.CostEstimate(flops=1 << 31, bytes_accessed=1 << 20, transcendentals=0),
        )()

    def __call__(self, body, outs, ins, late=(), scratch=(), left=(), onto=()):
        late = [item if isinstance(item, tuple) else (item, None) for item in late]
        far, near, given = len(late), len(ins), len(outs)

        def kernel(*refs):
            views = [View(ref, pick) for ref, (_, pick) in zip(refs, late, strict=False)]
            rest = refs[far + near + 1 :]
            body(*views, *refs[far : far + near], *rest[:given], *rest[given + 1 :])

        result = pl.pallas_call(
            kernel,
            name=getattr(body, "func", body).__name__,
            in_specs=[VMEM] * far
            + [ANY if i in onto else VMEM for i in range(near)]
            + [ANY],
            out_specs=[ANY if i in left else VMEM for i in range(given)] + [ANY],
            out_shape=[*outs, shape(self.token.shape)],
            scratch_shapes=list(scratch),
            input_output_aliases={far + i: o for i, o in zip(onto, left, strict=False)},
            compiler_params=pltpu.CompilerParams(vmem_limit_bytes=VMEM_BYTES),
            cost_estimate=pl.CostEstimate(flops=1024, bytes_accessed=1024, transcendentals=0),
        )(*(a for a, _ in late), *ins, self.token)
        self.token = result[-1]
        return result[:-1]


def hand_out(value, keep, send):
    size = keep.shape[0]
    for core in range(2):

        @pl.when(core_bit() == core)
        def _(core=core):
            keep[...] = value[core * size : (core + 1) * size]
            at = (1 - core) * size
            for ref in send:
                ref[...] = value[at : at + ref.shape[0]]
                at += ref.shape[0]


def chip_sum(keep, *refs):
    *got, out = refs
    size = got[0].shape[0]
    for i, ref in enumerate(got):
        at = slice(i * size, (i + 1) * size)
        out[at, :] = keep[at, :] + ref[...]


def total_sum(chip, far, *outs):
    size = outs[0].shape[0]
    for i, ref in enumerate(outs):
        at = slice(i * size, (i + 1) * size)
        ref[...] = chip[at, :] + far[at, :]


def gathered(parts, place):
    size, piece = place.shape[0] // 2, parts[0].shape[0]
    core = core_bit()
    for side, own in ((core, parts[: len(parts) // 2]), (1 - core, parts[len(parts) // 2 :])):
        for i, ref in enumerate(own):
            place[pl.ds(pl.multiple_of(side * size + i * piece, piece), piece), :] = ref[...]
    return place[...]


def head_lanes(size, heads, dim, h):
    lane = lax.broadcasted_iota(jnp.int32, (size, heads * dim), 1)
    return (lane >= h * dim) & (lane < (h + 1) * dim)


def attend(row, lens, tokens, groups, key_mask, wq, bq, wk, wv, bv, rel, wo, ctx, qo, ko, vo, prob, pooled_out, keep, *send):
    heads, table = rel.shape
    seq = tokens.shape[0]
    half = seq // 2
    dim = wq.shape[0] // heads
    tok = tokens[...]
    i = lax.broadcasted_iota(jnp.int32, (half, seq), 0)
    j = lax.broadcasted_iota(jnp.int32, (half, seq), 1)
    pick = jnp.where((j >> 1) == i, 0.5, 0.0).astype(BF16)
    pooled = nn(pick, tok)
    pooled_out[...] = pooled
    q = (nt(pooled.astype(BF16), wq[...]) + bq[...]).astype(BF16)
    k = nt(tok, wk[...]).astype(BF16)
    v = (nt(tok, wv[...]) + bv[...]).astype(BF16)
    qo[...] = q
    ko[...] = k
    vo[...] = v
    self_key = j == 2 * i
    group = groups[row : row + 1, :].astype(F32)
    place = lax.broadcasted_iota(jnp.int32, (1, seq), 1)
    live = (place < lens[...][:, row : row + 1]) & (key_mask[row : row + 1, :] == 1)
    own = jnp.sum(jnp.where(self_key, group, 0.0), axis=1, keepdims=True)
    allowed = self_key | (own == jnp.where(live, group, -1.0))
    out = jnp.zeros((half, heads * dim), F32)
    for h in range(heads):
        span = 2 * seq
        wing = (span - table) // 2
        low = rel[h : h + 1, : table // 2]
        high = rel[h : h + 1, table // 2 :]
        line = jnp.concatenate(
            [
                high,
                jnp.broadcast_to(rel[h : h + 1, table - 1 :], (1, wing)),
                jnp.broadcast_to(rel[h : h + 1, :1], (1, wing)),
                low,
            ],
            axis=1,
        )
        bias = pltpu.roll(jnp.broadcast_to(line, (half, span)), 0, 1, stride=2, stride_axis=0)[:, :seq]
        raw = nt(jnp.where(head_lanes(half, heads, dim, h), q, 0), k) * 0.125 + bias
        score = jnp.where(allowed, raw, -1e30)
        expo = jnp.exp(score - jnp.max(score, axis=1, keepdims=True))
        p = expo * (1.0 / jnp.sum(expo, axis=1, keepdims=True))
        prob[h] = p
        out = out + nn(p.astype(BF16), jnp.where(head_lanes(seq, heads, dim, h), v, 0))
    low_out = out.astype(BF16)
    ctx[...] = low_out
    hand_out(nn(low_out, wo[...]), keep, send)


def normalise(value):
    centre = value - jnp.mean(value, axis=1, keepdims=True)
    factor = lax.rsqrt(jnp.mean(centre * centre, axis=1, keepdims=True) + 1e-05)
    return centre * factor, factor


def forward(count, b_out, gain, shift, wi, bi, wt, pooled, *refs):
    parts, refs = refs[:count], refs[count:]
    normed_o, factor_o, ylow_o, act_o, slope_o, keep, *send, place = refs
    first = pooled[...] + (gathered(parts, place) + b_out[...])
    normed, factor = normalise(first)
    normed_o[...] = normed
    factor_o[...] = factor
    y_low = (normed * gain[...] + shift[...]).astype(BF16)
    ylow_o[...] = y_low
    inner = nn(y_low, wi[...]) + bi[...]
    cdf = 0.5 + 0.5 * lax.erf(inner * 0.7071067811865476)
    slope_o[...] = cdf + inner * (0.3989422804014327 * jnp.exp(-0.5 * inner * inner))
    act = (inner * cdf).astype(BF16)
    act_o[...] = act
    hand_out(nn(act, wt[...]), keep, send)


def norm_back(grad, normed, factor, gain):
    scaled = grad * gain
    one = jnp.mean(scaled, axis=1, keepdims=True)
    two = jnp.mean(scaled * normed, axis=1, keepdims=True)
    return factor * (scaled - one - normed * two)


def over_rows(value):
    return jnp.sum(value, axis=0, keepdims=True)


def turn(row, count, again, gain_one, shift_one, b_outer, gain, shift, cot, wt, wi, normed_one, slope, *refs):
    parts, refs = refs[:count], refs[count + again :]
    result, g_second_o, g_ffn_o, g_inner_o, small, keep, *send, place, low, done = refs
    y_one = normed_one[...] * gain_one[...] + shift_one[...]
    second = y_one + (gathered(parts, place) + b_outer[...])
    normed, factor = normalise(second)
    low[...] = (normed * gain[...] + shift[...]).astype(BF16)
    leave = pltpu.make_async_copy(low, result.at[row], done)
    leave.start()
    g_out = cot[...].astype(F32)
    g_second = norm_back(g_out, normed, factor, gain[...])
    g_second_o[...] = g_second
    g_ffn = g_second.astype(BF16)
    g_ffn_o[...] = g_ffn
    g_inner = (nt(g_ffn, wt[...]) * slope[...]).astype(BF16)
    g_inner_o[...] = g_inner
    hand_out(nt(g_inner, wi[...]), keep, send)
    small[0:1, :] = over_rows(g_inner.astype(F32))
    small[1:2, :] = over_rows(g_second)
    small[2:3, :] = over_rows(g_out * normed)
    small[3:4, :] = over_rows(g_out)
    leave.wait()


def ffn_weights(kind, lo, hi, act0, act1, g_ffn0, g_ffn1, y0, y1, g_in0, g_in1, *outs):
    def block(ref, lhs0, lhs1, rhs0, rhs1):
        ref[...] = tn(lhs0[:, lo:hi], rhs0[...]) + tn(lhs1[:, lo:hi], rhs1[...])

    outer = (act0, act1, g_ffn0, g_ffn1)
    inner = (y0, y1, g_in0, g_in1)
    if kind == "Z":
        block(outs[0].at[0], *outer)
        block(outs[0].at[1], *inner)
        return
    keep, send = outs

    @pl.when(x_bit() == 0)
    def _():
        block(keep, *outer)
        block(send, *inner)

    @pl.when(x_bit() != 0)
    def _():
        block(keep, *inner)
        block(send, *outer)


def attend_back(heads, count, gain, wo, wq, wk, wv, g_second, normed, factor, q_r, k_r, v_r, prob, *refs):
    parts, refs = refs[:count], refs[count:]
    g_first_o, g_attn_o, gs_o, gq_o, gk_o, gv_o, small, keep, *send, place = refs
    g_y = g_second[...] + gathered(parts, place)
    small[0:1, :] = over_rows(g_y * normed[...])
    small[1:2, :] = over_rows(g_y)
    g_first = norm_back(g_y, normed[...], factor[...], gain[...])
    g_first_o[...] = g_first
    small[2:3, :] = over_rows(g_first)
    g_attn = g_first.astype(BF16)
    g_attn_o[...] = g_attn
    g_ctx = nt(g_attn, wo[...]).astype(BF16)
    q, k, v = q_r[...], k_r[...], v_r[...]
    half, seq = q.shape[0], k.shape[0]
    dim = q.shape[1] // heads
    gq = jnp.zeros(q.shape, F32)
    gk = jnp.zeros(k.shape, F32)
    gv = jnp.zeros(k.shape, F32)
    for h in range(heads):
        own_q = head_lanes(half, heads, dim, h)
        own_k = head_lanes(seq, heads, dim, h)
        g_h = jnp.where(own_q, g_ctx, 0)
        p = prob[h]
        g_p = nt(g_h, v)
        g_s = (p * (g_p - jnp.sum(p * g_p, axis=1, keepdims=True))).astype(BF16)
        gs_o[h] = g_s
        gq = gq + nn(g_s, jnp.where(own_k, k, 0))
        gk = gk + tn(g_s, jnp.where(own_q, q, 0))
        gv = gv + tn(p.astype(BF16), g_h)
    gq = (gq * 0.125).astype(BF16)
    gk = (gk * 0.125).astype(BF16)
    gv = gv.astype(BF16)
    gq_o[...] = gq
    gk_o[...] = gk
    gv_o[...] = gv
    i = lax.broadcasted_iota(jnp.int32, (seq, half), 0)
    j = lax.broadcasted_iota(jnp.int32, (seq, half), 1)
    twice = jnp.where((i >> 1) == j, 0.5, 0.0).astype(BF16)
    gq_twice = nn(twice, gq).astype(BF16)
    hand_out(nn(gk, wk[...]) + nn(gv, wv[...]) + nn(gq_twice, wq[...]), keep, send)


def attn_weights_one(tokens, gq0, gq1, gv0, gv1, pooled0, pooled1, keep, send):
    def queries(ref):
        ref[...] = tn(gq0[...], pooled0[...].astype(BF16)) + tn(gq1[...], pooled1[...].astype(BF16))

    def values(ref):
        ref[...] = tn(gv0[...], tokens[0]) + tn(gv1[...], tokens[1])

    @pl.when(x_bit() == 0)
    def _():
        queries(keep)
        values(send)

    @pl.when(x_bit() != 0)
    def _():
        values(keep)
        queries(send)


def attn_weights_two(heads, table, tokens, gq0, gq1, gk0, gk1, gv0, gv1, ctx0, ctx1, ga0, ga1, gs0, gs1, t0, t1, a0, a1, keep, send):
    seq = tokens.shape[1]
    half, e = gq0.shape
    width = tokens.shape[2]
    i = lax.broadcasted_iota(jnp.int32, (half, half), 0)
    j = lax.broadcasted_iota(jnp.int32, (half, half), 1)
    flip = jnp.where(i + j == half - 1, 1.0, 0.0).astype(BF16)
    lane = lax.broadcasted_iota(jnp.int32, (1, table // 2), 1)
    span = 2 * seq
    pieces = []
    for h in range(heads):
        score = nn(flip, gs0[h]) + nn(flip, gs1[h])
        score = jnp.concatenate([score, jnp.zeros_like(score)], axis=1)
        along = over_rows(pltpu.roll(score, span - 2 * (half - 1), 1, stride=2, stride_axis=0))
        lo = jnp.sum(along[:, seq : span - table // 2], axis=1, keepdims=True)
        hi = jnp.sum(along[:, table // 2 : seq], axis=1, keepdims=True)
        pieces.append(along[:, span - table // 2 :] + jnp.where(lane == 0, lo, 0.0))
        pieces.append(along[:, : table // 2] + jnp.where(lane == table // 2 - 1, hi, 0.0))
    small = [t0[r : r + 1, :] + t1[r : r + 1, :] for r in range(4)]
    small += [a0[r : r + 1, :] + a1[r : r + 1, :] for r in range(3)]
    small.append(jnp.concatenate(pieces, axis=1))
    bq = over_rows(gq0[...].astype(F32)) + over_rows(gq1[...].astype(F32))
    bv = over_rows(gv0[...].astype(F32)) + over_rows(gv1[...].astype(F32))
    last = jnp.concatenate([bq, bv, jnp.zeros((1, width - 2 * e), F32)], axis=1)

    def keys(ref):
        ref[:e, :] = tn(gk0[...], tokens[0]) + tn(gk1[...], tokens[1])
        for r, value in enumerate(small):
            ref[e + r : e + r + 1, :] = value

    def outs(ref):
        ref[:e, :] = tn(ctx0[...], ga0[...]) + tn(ctx1[...], ga1[...])
        ref[e:, :] = jnp.broadcast_to(last, (ref.shape[0] - e, width))

    @pl.when(x_bit() == 0)
    def _():
        keys(keep)
        outs(send)

    @pl.when(x_bit() != 0)
    def _():
        outs(keep)
        keys(send)


def token_end(row, count, again, g_first, *refs):
    parts, refs = refs[:count], refs[count + again :]
    result, place, twice, out, done = refs
    total = gathered(parts, place)
    half = g_first.shape[0]
    for s in range(g_first.shape[1] // 128):
        at = slice(s * 128, (s + 1) * 128)
        value = g_first[:, at] * 0.5
        twice[pl.ds(0, half, stride=2), :] = value
        twice[pl.ds(1, half, stride=2), :] = value
        out[:, at] = (total[:, at] + twice[...]).astype(BF16)
    leave = pltpu.make_async_copy(out, result.at[row], done)
    leave.start()
    leave.wait()


def add(a, b, out):
    out[...] = a[...] + b[...]


def add_split(a, b, keep, send):
    own = centre_half()
    keep[...] = a[own] + b[own]
    send[...] = a[1 - own] + b[1 - own]


def choose(mine, got, out):
    @pl.when(in_centre())
    def _():
        out[...] = mine[...]

    @pl.when(jnp.logical_not(in_centre()))
    def _():
        out[...] = got[...]


def ffn_end(kind, lo, count, *refs):
    parts, (outer, inner, *sems) = refs[:count], refs[-4:]

    def lay(which, low, high):
        @pl.when(which)
        def _():
            copies = [
                pltpu.make_async_copy(part, out.at[lo : lo + part.shape[0]], sem)
                for part, out, sem in zip((low, high), (outer, inner), sems, strict=True)
            ]
            for copy in copies:
                copy.start()
            for copy in copies:
                copy.wait()

    if kind == "X":
        lay(x_bit() == 0, parts[0], parts[1])
        lay(x_bit() != 0, parts[1], parts[0])
        return
    if kind == "V":
        for here, far in ((in_centre(), parts[2]), (jnp.logical_not(in_centre()), parts[1])):
            lay(here & (x_bit() == 0), parts[0], far)
            lay(here & (x_bit() != 0), far, parts[0])
        return
    for here, one, two in ((in_centre(), *parts[:2]), (jnp.logical_not(in_centre()), *parts[2:])):
        lay(here & (centre_half() == 0), one, two)
        lay(here & (centre_half() == 1), two, one)


def attn_end_one(final, far, wq, wv):
    def lay(query, value):
        wq[...] = query[...]
        wv[...] = value[...]

    @pl.when(x_bit() == 0)
    def _():
        lay(final, far)

    @pl.when(x_bit() != 0)
    def _():
        lay(far, final)


def attn_end_two(final, far, wk, wo, bq, bv, rel, *small):
    e, width = wk.shape
    heads = rel.shape[0]
    table = width // heads

    def lay(one, two):
        wk[...] = one[:e, :]
        wo[...] = two[:e, :]
        for r, ref in enumerate(small):
            ref[...] = one[e + r, :]
        for h in range(heads):
            rel[h : h + 1, :] = one[e + len(small) : e + len(small) + 1, h * table : (h + 1) * table]
        bq[...] = two[e, :e]
        bv[...] = two[e, e : 2 * e]

    @pl.when(x_bit() == 0)
    def _():
        lay(final, far)

    @pl.when(x_bit() != 0)
    def _():
        lay(far, final)


CHUNKS = [("X", 0, 2), ("V", 2, 4), ("X", 4, 5), ("Z", 5, 6)]


class TensorSum:
    def __init__(self, run, keep, *send):
        self.run, self.keep, self.got = run, keep, [core_swap(a) for a in send]

    def add(self):
        (self.chip,) = self.run(chip_sum, [shape(self.keep.shape)], [self.keep, *self.got])
        self.far = chip_swap(self.chip)

    def tot(self):
        mine = self.run(total_sum, [shape(a.shape) for a in self.got], [self.chip, self.far])
        self.parts = [*mine, *(core_swap(a) for a in mine)]


def others(a, bit):
    while bit < lax.axis_size("dp"):
        a = a + lax.ppermute(a, "dp", swap_pairs(lax.axis_size("dp"), bit))
        bit *= 2
    return a


class XFirst:
    def __init__(self, run, make):
        self.run, self.make_outs = run, make

    def plus(self, pairs):
        (self.mine,) = self.run(add, [shape(self.mine.shape)], [self.mine, self.got])
        self.got = hop(self.mine, pairs) if on_line_of_four() else None

    def make(self):
        self.mine, send = self.make_outs()
        self.got = x_swap(send)

    def xa(self):
        self.plus(INWARD)

    def ia(self):
        if on_line_of_four():
            self.plus(MIDDLE)

    def ma(self):
        if on_line_of_four():
            self.plus(OUTWARD)

    def ch(self):
        if on_line_of_four():
            (self.mine,) = self.run(choose, [shape(self.mine.shape)], [self.mine, self.got])
        else:
            self.mine = others(self.mine, 2)
        self.parts = [self.mine, x_swap(self.mine)]


class XOuter(XFirst):
    def ch(self):
        if not on_line_of_four():
            super().ch()
            self.parts.append(self.parts[1])
            return
        (self.mine,) = self.run(choose, [shape(self.mine.shape)], [self.mine, self.got])
        other = hop(self.mine, OUTER_X)
        self.parts = [self.mine, other, hop(other, INWARD)]


class ZFirst:
    def __init__(self, run, make):
        self.run, self.make_outs = run, make

    def make(self):
        (self.whole,) = self.make_outs()
        self.got = hop(self.whole, INWARD) if on_line_of_four() else None

    def ia(self):
        if on_line_of_four():
            half = shape(self.whole.shape[1:])
            self.mine, send = self.run(add_split, [half, half], [self.whole, self.got])
            self.got = hop(send, MIDDLE)

    def ma(self):
        if on_line_of_four():
            (self.mine,) = self.run(add, [shape(self.mine.shape)], [self.mine, self.got])
            self.got = hop(self.mine, CENTRE_X)

    def xa(self):
        if on_line_of_four():
            (mine,) = self.run(add, [shape(self.mine.shape)], [self.mine, self.got])
            other = hop(mine, MIDDLE)
            self.parts = [mine, other, hop(mine, OUTWARD), hop(other, OUTWARD)]
        else:
            total, own = others(self.whole, 1), centre_half() == 0
            pair = [jnp.where(own, total[0], total[1]), jnp.where(own, total[1], total[0])]
            self.parts = pair + pair


def local(
    tokens,
    lengths,
    groups,
    key_mask,
    w_query,
    b_query,
    w_key,
    w_value,
    b_value,
    rel_bias,
    w_out,
    b_out,
    gain_one,
    shift_one,
    w_inner,
    b_inner,
    w_outer,
    b_outer,
    gain_two,
    shift_two,
    cotangent,
):
    rows, seq, width = tokens.shape
    half = seq // 2
    heads, table = rel_bias.shape
    e = w_query.shape[1]
    hidden = w_inner.shape[1]
    w_query, w_key, w_value = w_query.T, w_key.T, w_value.T
    run = Line()
    place = lambda n: pltpu.VMEM((n, width), F32)
    dma = pltpu.SemaphoreType.DMA

    def summands(n, piece=PIECE):
        return [shape((n // 2, width))] + [shape((piece, width))] * (n // 2 // piece)

    class Row:
        output = grad_tokens = None

        def __init__(self, r):
            self.r = r

        def attend(self):
            outs = [
                shape((half, e), BF16),
                shape((half, e), BF16),
                shape((seq, e), BF16),
                shape((seq, e), BF16),
                shape((heads, half, seq)),
                shape((half, width)),
            ]
            late = [lengths, (tokens, self.r), groups, key_mask]
            late += [w_query, b_query, w_key, w_value, b_value, rel_bias, w_out]
            got = run(functools.partial(attend, self.r), outs + summands(half), [], late=late)
            self.ctx, self.q, self.k, self.v, self.prob, self.pooled = got[:6]
            self.att = TensorSum(run, *got[6:])

        def forward(self):
            outs = [
                shape((half, width)),
                shape((half, 1)),
                shape((half, width), BF16),
                shape((half, hidden), BF16),
                shape((half, hidden)),
            ]
            parts = self.att.parts
            got = run(
                functools.partial(forward, len(parts)),
                outs + summands(half),
                [self.pooled, *parts],
                late=[b_out, gain_one, shift_one, w_inner, b_inner, w_outer],
                scratch=[place(half)],
            )
            self.normed, self.factor, self.y_low, self.act, self.slope = got[:5]
            self.ffn = TensorSum(run, *got[5:])

        def turn(self):
            outs = [
                shape((rows, half, width), BF16),
                shape((half, width)),
                shape((half, width), BF16),
                shape((half, hidden), BF16),
                shape((8, width)),
            ]
            parts = self.ffn.parts
            before = [] if Row.output is None else [Row.output]
            got = run(
                functools.partial(turn, self.r, len(parts), len(before)),
                outs + summands(half),
                [self.normed, self.slope, *parts, *before],
                late=[gain_one, shift_one, b_outer, gain_two, shift_two, (cotangent, self.r), w_outer, w_inner],
                scratch=[place(half), pltpu.VMEM((half, width), BF16), dma],
                left=(0,),
                onto=[2 + len(parts)] if before else (),
            )
            Row.output, self.g_second, self.g_ffn, self.g_inner, self.t_small = got[:5]
            self.back = TensorSum(run, *got[5:])

        def aback(self):
            outs = [
                shape((half, width)),
                shape((half, width), BF16),
                shape((heads, half, seq), BF16),
                shape((half, e), BF16),
                shape((seq, e), BF16),
                shape((seq, e), BF16),
                shape((8, width)),
            ]
            parts = self.back.parts
            got = run(
                functools.partial(attend_back, heads, len(parts)),
                outs + summands(seq, seq // 2),
                [self.g_second, self.normed, self.factor, self.q, self.k, self.v, self.prob, *parts],
                late=[gain_one, w_out, w_query, w_key, w_value],
                scratch=[place(half)],
            )
            self.g_first, self.g_attn, self.gs, self.gq, self.gk, self.gv, self.a_small = got[:7]
            self.tok = TensorSum(run, *got[7:])

        def tokend(self):
            parts = self.tok.parts
            before = [] if Row.grad_tokens is None else [Row.grad_tokens]
            (Row.grad_tokens,) = run(
                functools.partial(token_end, self.r, len(parts), len(before)),
                [shape((rows, seq, width), BF16)],
                [self.g_first, *parts, *before],
                scratch=[place(seq), pltpu.VMEM((seq, 128), F32), pltpu.VMEM((seq, width), BF16), dma],
                left=(0,),
                onto=[1 + len(parts)] if before else (),
            )

    r0, r1 = (Row(r) for r in range(rows))

    def ffn_chunk(kind, lo, hi):
        def make():
            outs = [shape((2, hi - lo, width))] if kind == "Z" else [shape((hi - lo, width))] * 2
            ins = [r0.act, r1.act, r0.g_ffn, r1.g_ffn, r0.y_low, r1.y_low, r0.g_inner, r1.g_inner]
            return run(functools.partial(ffn_weights, kind, lo, hi), outs, ins)

        return {"X": XFirst, "V": XOuter, "Z": ZFirst}[kind](run, make)

    cuts = [(kind, lo * width // 6, hi * width // 6) for kind, lo, hi in CHUNKS]
    chunks = [ffn_chunk(*cut) for cut in cuts]
    x, v, z = ([chunk for chunk in chunks if type(chunk) is kind] for kind in (XFirst, XOuter, ZFirst))

    def attn_one():
        ins = [tokens, r0.gq, r1.gq, r0.gv, r1.gv, r0.pooled, r1.pooled]
        return run(attn_weights_one, [shape((e, width))] * 2, ins)

    def attn_two():
        ins = [tokens, r0.gq, r1.gq, r0.gk, r1.gk, r0.gv, r1.gv, r0.ctx, r1.ctx, r0.g_attn, r1.g_attn]
        ins += [r0.gs, r1.gs, r0.t_small, r1.t_small, r0.a_small, r1.a_small]
        return run(functools.partial(attn_weights_two, heads, table), [shape((e + 8, width))] * 2, ins)

    a = [XFirst(run, attn_one), XFirst(run, attn_two)]

    class Ffn:
        grads = ()

    def end(chunk):
        cut = cuts[chunks.index(chunk)]
        outs = [shape((hidden, width)), shape((width, hidden))]
        count = len(chunk.parts)
        Ffn.grads = run(
            functools.partial(ffn_end, *cut[:2], count),
            outs,
            [*chunk.parts, *Ffn.grads],
            scratch=[dma, dma],
            left=(0, 1),
            onto=[count, count + 1] if Ffn.grads else (),
        )

    def aend0():
        return run(attn_end_one, [shape((e, width))] * 2, a[0].parts)

    def aend1():
        outs = [shape((e, width))] * 2 + [shape((e,)), shape((e,)), shape((heads, table))] + [shape((width,))] * 7
        return run(attn_end_two, outs, a[1].parts)

    r0.attend()
    r0.att.add()
    r1.attend()
    r1.att.add()
    r0.att.tot()
    r0.forward()
    r0.ffn.add()
    r1.att.tot()
    r1.forward()
    r1.ffn.add()
    r0.ffn.tot()
    r0.turn()
    r0.back.add()
    r1.ffn.tot()
    r1.turn()
    v[0].make()
    z[0].make()
    x[0].make()
    r0.back.tot()
    r0.aback()
    r1.back.add()
    v[0].xa()
    r1.back.tot()
    z[0].ia()
    r1.aback()
    r0.tok.add()
    a[0].make()
    x[0].xa()
    z[0].ma()
    v[0].ia()
    a[1].make()
    x[1].make()
    r0.tok.tot()
    a[0].xa()
    r1.tok.add()
    x[0].ia()
    v[0].ma()
    a[1].xa()
    a[0].ia()
    r1.tok.tot()
    x[0].ma()
    x[1].xa()
    v[0].ch()
    a[1].ia()
    a[0].ma()
    z[0].xa()
    x[1].ia()
    x[0].ch()
    a[1].ma()
    a[0].ch()
    r0.tokend()
    end(x[0])
    x[1].ma()
    end(v[0])
    a[1].ch()
    x[1].ch()
    grad_w_query, grad_w_value = aend0()
    grad_w_key, grad_w_out, grad_b_query, grad_b_value, grad_rel_bias, *small = aend1()
    end(z[0])
    r1.tokend()
    end(x[1])
    grad_w_outer, grad_w_inner = Ffn.grads
    grad_b_inner, grad_b_outer, grad_gain_two, grad_shift_two, grad_gain_one, grad_shift_one, grad_b_out = small
    return (
        Row.output,
        Row.grad_tokens,
        grad_w_query.T,
        grad_b_query,
        grad_w_key.T,
        grad_w_value.T,
        grad_b_value,
        grad_rel_bias,
        grad_w_out,
        grad_b_out,
        grad_gain_one,
        grad_shift_one,
        grad_w_inner,
        grad_b_inner,
        grad_w_outer,
        grad_b_outer,
        grad_gain_two,
        grad_shift_two,
    )


def solution(mesh):
    placed = (
        P("dp", None, None),
        P("dp"),
        P("dp", None),
        P("dp", None),
        P(None, "tensor"),
        P("tensor"),
        P(None, "tensor"),
        P(None, "tensor"),
        P("tensor"),
        P("tensor", None),
        P("tensor", None),
        P(),
        P(),
        P(),
        P(None, "tensor"),
        P("tensor"),
        P("tensor", None),
        P(),
        P(),
        P(),
        P("dp", None, None),
    )
    return jax.shard_map(
        local,
        mesh=mesh,
        in_specs=placed,
        out_specs=(
            P("dp", None, None),
            P("dp", None, None),
            P(None, "tensor"),
            P("tensor"),
            P(None, "tensor"),
            P(None, "tensor"),
            P("tensor"),
            P("tensor", None),
            P("tensor", None),
            P(),
            P(),
            P(),
            P(None, "tensor"),
            P("tensor"),
            P("tensor", None),
            P(),
            P(),
            P(),
        ),
        check_vma=False,
    )
```
